512 devices in a mesh: req: 8 (over z_lo), section: 2 (over core), seq: 8 (over z_hi, y), tp: 4 (over x).
Axes of the slice: x: 4, y: 4, z: 16 (z_hi: 2, z_lo: 8; z = z_hi * 8 + z_lo), core: 2. Of those that a mesh axis runs over, the one named last changes fastest.
Arguments:
- hidden: bfloat16 [8192, 1536], P(('req', 'seq'), 'tp'), parts along dimension 0, may hold values from -2.5 to 2.5
- latent: float32 [8192, 64], P(('req', 'seq'), ('section', 'tp')), parts along dimension 0, may hold values from -6 to 6
- w_qkv: bfloat16 [2, 1536, 3, 1536], P('section', 'seq', None, 'tp'), may hold values from -0.15625 to 0.15625
- w_out: bfloat16 [2, 1536, 1536], P('section', 'tp'), may hold values from -0.625 to 0.625
- modulation: float32 [2, 3, 1536], P('section'), may hold values from -3 to 3
- final_mod: float32 [2, 1536], replicated, may hold values from -3 to 3
- w_final: bfloat16 [1536, 64], P(None, ('section', 'tp')), may hold values from -0.15625 to 0.15625
- stale_kv: bfloat16 [2, 2, 8192, 1536], P('section', None, ('req', 'seq'), 'tp'), parts along dimension 2, may hold values from -6 to 6
- text_kv: bfloat16 [2, 2, 1232, 1536], P('section', None, 'req', 'tp'), parts along dimension 2, as said below
- text_len: int32 [8], P('req'), parts along dimension 0, may hold values from 77 to 154
- patch_order: int32 [64, 4], P('req'), parts along dimension 0, may hold values from 0 to 3, each once within a row
- step_size: float32 [1], replicated, may hold values from -0.6 to -0.1
Outputs:
- latent_next: float32 [8192, 64], P(('req', 'seq'), ('section', 'tp')), parts along dimension 0
- new_kv: bfloat16 [2, 2, 8192, 1536], P('section', None, ('req', 'seq'), 'tp'), parts along dimension 2
The draws below stay inside these ranges and needn't reach their ends.
There are 8 independent parts, one for each index of `req`. The reference program is written for one: setup_inputs(seed, part) draws one part's arguments, and reference() takes and returns one part's arrays. A program takes and returns all parts, laid end to end along the dimension named above; an argument that names none is the same for every part. Nothing has to cross between parts.
Inputs may be any that keep to these rules, and one draw needn't show every extreme that they name: Text tokens 0 to text_len - 1 are live, the rest of the 154 slots are padding. `patch_order`: each row is an ordering of the 4 patches of one index of seq. `text_kv`: keys and values of the text tokens.
All inputs are finite; a program needn't handle non-finite values.
Results may differ from the reference program's by a relative error of at most 0.015.
The reference program's roundings to bfloat16 on the way count: a program that leaves them out, or rounds other values in their place, can miss the bound.
Values may be sent and summed in bfloat16 or wider, within the bound.
A program may use at most 64 MiB of HBM per device.

```python
import jax
import jax.numpy as jnp
from jax import lax

D = 1536
HEADS = 24
HEAD = 64
CH = 64
TEXT = 154
MICRO = 4
PATCH = 32
IMG = 1024
LAYERS = 2
N_SEQ = 8


def draw_text_kv(key, part):
    base_key = jax.random.fold_in(key, 0)
    array_shape = (LAYERS, 2, TEXT, D)
    values = jax.random.normal(base_key, array_shape, jnp.float32)
    return values.astype(jnp.bfloat16)


def levels(key, dims, cuts, least, largest):
    gain, own = 1.0, jax.random.fold_in(key, 6)
    for position, shards_of in cuts:
        heights = jnp.exp(jax.random.uniform(jax.random.fold_in(own, position), (shards_of,), jnp.float32, least / len(cuts), largest / len(cuts)))
        gain = gain * jnp.repeat(heights, dims[position] // shards_of).reshape([-1 if axis == position else 1 for axis in range(len(dims))])
    return gain


def normal_values(own_key, shape, deviation, reach, shards=(), kind=jnp.bfloat16):
    values = deviation * jax.random.normal(own_key, shape, jnp.float32)
    if shards:
        values = values * levels(own_key, shape, shards, -0.22, 0.18)
    return jnp.clip(values, -reach, reach).astype(kind)


def setup_inputs(seed: int = 0, part: int = 0) -> dict:
    key_of = jax.random.split(jax.random.key(seed), 13)
    part_splits = jax.random.split(jax.random.fold_in(key_of[12], part), 13)
    hidden = normal_values(part_splits[0], (IMG, D), 0.25, 2.5, ((0, 8), (1, 4)))
    latent = normal_values(part_splits[1], (IMG, CH), 1.0, 6.0, ((0, 8), (1, 8)), jnp.float32)
    w_qkv = normal_values(key_of[2], (LAYERS, D, 3, D), D ** -0.5, 0.15625, ((0, 2), (1, 8), (3, 4)))
    w_out = normal_values(key_of[3], (LAYERS, D, D), (D // 16) ** -0.5, 0.625, ((0, 2), (1, 4)))
    modulation = normal_values(key_of[4], (LAYERS, 3, D), 0.5, 3.0, ((0, 2),), jnp.float32)
    final_mod = normal_values(key_of[5], (2, D), 0.5, 3.0, (), jnp.float32)
    w_final = normal_values(key_of[6], (D, CH), D ** -0.5, 0.15625, ((1, 8),))
    stale_kv = normal_values(part_splits[7], (LAYERS, 2, IMG, D), 1.0, 6.0, ((0, 2), (2, 8), (3, 4)))
    text_kv = draw_text_kv(jax.random.fold_in(jax.random.fold_in(key_of[12], part), 71), part)
    text_len = jax.random.randint(part_splits[9], (1,), TEXT // 2, TEXT + 1).astype(jnp.int32)
    patch_order = jax.vmap(lambda own: jax.random.permutation(own, MICRO))(jax.random.split(part_splits[10], N_SEQ)).reshape((N_SEQ, MICRO)).astype(jnp.int32)
    step_size = jnp.clip(jax.random.uniform(key_of[11], (1,), jnp.float32, -0.6, -0.1), -0.6, -0.1)
    return dict(hidden=hidden, latent=latent, w_qkv=w_qkv, w_out=w_out, modulation=modulation, final_mod=final_mod, w_final=w_final, stale_kv=stale_kv, text_kv=text_kv, text_len=text_len, patch_order=patch_order, step_size=step_size)


def layer_norm(row_block):
    row_block = row_block.astype(jnp.float32)
    center = row_block - lax.optimization_barrier(jnp.mean(row_block, axis=-1, keepdims=True))
    spread = lax.optimization_barrier(jnp.mean(center * center, axis=-1, keepdims=True))
    return center * lax.rsqrt(spread + 1e-06)

def modulate(row_block, shift_vec, scale_vec):
    return (layer_norm(row_block) * (1.0 + scale_vec) + shift_vec).astype(jnp.bfloat16)

def attention(queries, all_keys, all_values, text_keys, text_values, live_mask):

    def split_heads(array_in):
        return array_in.reshape(array_in.shape[0], HEADS, HEAD).transpose(1, 0, 2)
    factor = HEAD ** (-0.5)

    def one_head(head_parts):
        q_head, k_head, v_head, tk_head, tv_head = head_parts
        scores = jnp.dot(q_head, k_head.T, preferred_element_type=jnp.float32) * factor
        text_scores = jnp.dot(q_head, tk_head.T, preferred_element_type=jnp.float32) * factor
        text_scores = jnp.where(live_mask[None, :], text_scores, -jnp.inf)
        peak_score = jnp.maximum(lax.optimization_barrier(jnp.max(scores, axis=-1, keepdims=True)), lax.optimization_barrier(jnp.max(text_scores, axis=-1, keepdims=True)))
        weights = jnp.exp(scores - peak_score)
        text_weights = jnp.exp(text_scores - peak_score)
        total_mass = lax.optimization_barrier(jnp.sum(weights, axis=-1, keepdims=True)) + lax.optimization_barrier(jnp.sum(text_weights, axis=-1, keepdims=True))
        prob_img = (weights / total_mass).astype(jnp.bfloat16)
        text_probs = (text_weights / total_mass).astype(jnp.bfloat16)
        head_out = jnp.dot(prob_img, v_head, preferred_element_type=jnp.float32)
        return head_out + jnp.dot(text_probs, tv_head, preferred_element_type=jnp.float32)
    head_outs = lax.map(one_head, (split_heads(queries), split_heads(all_keys), split_heads(all_values), split_heads(text_keys), split_heads(text_values)))
    return head_outs.transpose(1, 0, 2).reshape(-1, D).astype(jnp.bfloat16)

def reference(hidden, latent, w_qkv, w_out, modulation, final_mod, w_final, stale_kv, text_kv, text_len, patch_order, step_size):
    micro_ids = jnp.arange(MICRO, dtype=jnp.int32)
    patch_rank = lax.optimization_barrier(jnp.sum(jnp.where(patch_order[:, :, None] == micro_ids[None, None, :], micro_ids[None, :, None], 0), axis=1))
    row_rank = jnp.repeat(patch_rank.reshape(-1), PATCH)
    live_mask = jnp.arange(TEXT, dtype=jnp.int32) < text_len[0]
    hidden_now = hidden
    fresh_all = []
    for layer_index in range(LAYERS):
        shift_vec = modulation[layer_index, 0]
        scale_vec = modulation[layer_index, 1]
        gate_vec = modulation[layer_index, 2]
        normed = modulate(hidden_now, shift_vec, scale_vec)
        joined = jnp.dot(normed, w_qkv[layer_index].reshape(D, 3 * D), preferred_element_type=jnp.float32).astype(jnp.bfloat16)
        queries = joined[:, :D]
        new_keys = joined[:, D:2 * D]
        new_values = joined[:, 2 * D:]
        fresh_all.append(jnp.stack([new_keys, new_values]))
        query_blocks = queries.reshape(N_SEQ, MICRO, PATCH, D)
        hidden_blocks = hidden_now.reshape(N_SEQ, MICRO, PATCH, D)
        layer_out = hidden_blocks
        for micro_step in range(MICRO):
            fresh_mask = (row_rank <= micro_step)[:, None]
            eff_keys = jnp.where(fresh_mask, new_keys, stale_kv[layer_index, 0])
            eff_values = jnp.where(fresh_mask, new_values, stale_kv[layer_index, 1])
            chosen = patch_order[:, micro_step]
            picked = micro_ids[None, :] == chosen[:, None]
            picked_queries = lax.optimization_barrier(jnp.sum(jnp.where(picked[:, :, None, None], query_blocks, jnp.zeros_like(query_blocks)), axis=1)).reshape(-1, D)
            picked_hidden = lax.optimization_barrier(jnp.sum(jnp.where(picked[:, :, None, None], hidden_blocks, jnp.zeros_like(hidden_blocks)), axis=1)).reshape(-1, D)
            attended = attention(picked_queries, eff_keys, eff_values, text_kv[layer_index, 0], text_kv[layer_index, 1], live_mask)
            branch = jnp.dot(attended, w_out[layer_index], preferred_element_type=jnp.float32)
            updated = (picked_hidden.astype(jnp.float32) + gate_vec * branch).astype(jnp.bfloat16).reshape(N_SEQ, PATCH, D)
            layer_out = jnp.where(picked[:, :, None, None], updated[:, None], layer_out)
        hidden_now = layer_out.reshape(IMG, D)
    final = modulate(hidden_now, final_mod[0], final_mod[1])
    velocity = jnp.dot(final, w_final, preferred_element_type=jnp.float32)
    latent_next = latent + step_size[0] * velocity
    return (latent_next, jnp.stack(fresh_all))
```

```python
import jax
import jax.numpy as jnp
from jax import lax
from jax.experimental import pallas as pl
from jax.experimental.pallas import tpu as pltpu
from jax.sharding import PartitionSpec as P

HEAD = 64
MICRO = 4
NC = 4
MESH = pl.DeviceIdType.MESH
F32 = jnp.float32
BF16 = jnp.bfloat16


def dot(a, b):
    return jnp.dot(a, b, preferred_element_type=F32)


def dot_nt(a, b):
    return lax.dot_general(a, b, (((1,), (1,)), ((), ())), preferred_element_type=F32)


class Link:
    def __init__(self, send_sem, recv_sem):
        self.send_sem, self.recv_sem, self.used = send_sem, recv_sem, 0

    def take(self):
        index = self.used
        self.used += 1
        return index

    def make(self, index, src, dst, device):
        return pltpu.make_async_remote_copy(
            src_ref=src,
            dst_ref=dst,
            send_sem=self.send_sem.at[index],
            recv_sem=self.recv_sem.at[index],
            device_id=device,
            device_id_type=MESH,
        )


N_LINK = 64
N_LOCAL = 5


def kernel(
    order, tlen, step, hid_h, w_h, wo_h, st_h, tx_h, mod, fmod, wf, lat,
    out_lat, out_kv,
    hx, wv, kvf, kvs, tx, wo, nm, at, lhs, nkv, fin, acc, sbuf,
    send_sem, recv_sem, loc_sem, go_sem,
):
    sec = lax.axis_index("section")
    seq = lax.axis_index("seq")
    tp = lax.axis_index("tp")
    req = lax.axis_index("req")
    zh = seq // 4
    oh = 1 - zh
    y = seq % 4
    z = zh * 8 + req
    far = req // 4
    hop = 1 - 2 * far
    depth = req + far * (7 - 2 * req)
    xs = [(tp + k) % 4 for k in (1, 2, 3)]
    ys = [(y + k) % 4 for k in (1, 2, 3)]
    xfrom = [(tp + 4 - k) % 4 for k in (1, 2, 3)]
    yfrom = [(y + 4 - k) % 4 for k in (1, 2, 3)]
    xdev = [{"tp": v} for v in xs]
    ydev = [{"seq": zh * 4 + v} for v in ys]
    zdev = {"seq": (seq + 4) % 8}
    core = {"section": 1 - sec}
    znext = (z + hop + 16) % 16
    zprev = (z - hop + 16) % 16
    next_dev = {"seq": (znext // 8) * 4 + y, "req": znext % 8}
    prev_dev = {"seq": (zprev // 8) * 4 + y, "req": zprev % 8}

    barrier = pltpu.get_barrier_semaphore()
    for device in xdev + ydev + [zdev, core, next_dev, prev_dev]:
        pl.semaphore_signal(barrier, inc=1, device_id=device, device_id_type=MESH)
    pl.semaphore_wait(barrier, 10)

    link = Link(send_sem, recv_sem)
    half_rows = lambda h: pl.ds(h * 128, 128)
    i_hx = [link.take() for _ in range(3)]
    i_hz = link.take()
    i_hf = [link.take() for _ in range(3)]
    i_wy = [link.take() for _ in range(3)]
    i_ch = [link.take() for _ in range(NC)]
    i_ex = [link.take() for _ in range(NC)]
    i_wr = [[link.take() for _ in range(3)] for _ in range(NC)]
    i_sy = [link.take() for _ in range(3)]
    i_sz = link.take()
    i_sr = [link.take() for _ in range(3)]
    i_wo = [link.take() for _ in range(3)]
    i_kv = [link.take() for _ in range(3)]
    i_nk = link.take()
    i_ax = [link.take() for _ in range(3)]
    i_az = link.take()
    i_af = [link.take() for _ in range(3)]
    i_h1 = [link.take() for _ in range(4)]
    i_fn = link.take()

    def send(index, src, dst, device):
        link.make(index, src, dst, device).start()

    def arrived(index, dst):
        link.make(index, dst, dst, core).wait_recv()

    def sent(index, src):
        link.make(index, src, src, core).wait_send()

    def local(index, src, dst):
        return pltpu.make_async_copy(src, dst, loc_sem.at[index])

    hx_slot = lambda x, h: hx.at[x, half_rows(h), :]

    def hidden_send():
        send(i_hz, hid_h, hx_slot(tp, zh), zdev)
        for k in range(3):
            send(i_hx[k], hid_h, hx_slot(tp, zh), xdev[k])
        local(0, hid_h, hx_slot(tp, zh)).start()

    def hidden_own():
        local(0, hid_h, hx_slot(tp, zh)).wait()
        for k in range(3):
            arrived(i_hx[k], hx_slot(xfrom[k], zh))

    def hidden_forward():
        arrived(i_hz, hx_slot(tp, oh))
        for k in range(3):
            send(i_hf[k], hx_slot(tp, oh), hx_slot(tp, oh), xdev[k])

    def hidden_other():
        for k in range(3):
            arrived(i_hf[k], hx_slot(xfrom[k], oh))

    def hidden_sent():
        sent(i_hz, hid_h)
        for k in range(3):
            sent(i_hx[k], hid_h)
            sent(i_hf[k], hx_slot(tp, oh))

    CR = 192 // NC
    w_rows = lambda s: wv.at[pl.ds(s * 192, 192), :]
    w_piece = lambda s, c: wv.at[pl.ds(s * 192 + c * CR, CR), :]

    def weights_send():
        @pl.when(depth == 0)
        def _():
            for c in range(NC):
                pltpu.make_async_remote_copy(
                    src_ref=w_h.at[oh, pl.ds(c * CR, CR), :],
                    dst_ref=w_piece(seq, c),
                    send_sem=send_sem.at[i_ex[c]],
                    recv_sem=recv_sem.at[i_ch[c]],
                    device_id=prev_dev,
                    device_id_type=MESH,
                ).start()

        for k in range(3):
            send(i_wy[k], w_h.at[zh], w_rows(seq), ydev[k])
        local(1, w_h.at[zh], w_rows(seq)).start()

    oseq = oh * 4 + y

    def weights_relay():
        for c in range(NC):
            arrived(i_ch[c], w_piece(oseq, c))

            @pl.when(depth < 3)
            def _(c=c):
                send(i_ch[c], w_piece(oseq, c), w_piece(oseq, c), next_dev)

            for k in range(3):
                send(i_wr[c][k], w_piece(oseq, c), w_piece(oseq, c), ydev[k])

    def weights_near():
        local(1, w_h.at[zh], w_rows(seq)).wait()
        for k in range(3):
            arrived(i_wy[k], w_rows(zh * 4 + yfrom[k]))

    def weights_far():
        for c in range(NC):
            for k in range(3):
                arrived(i_wr[c][k], w_piece(oh * 4 + yfrom[k], c))

    def weights_sent():
        @pl.when(depth == 0)
        def _():
            for c in range(NC):
                sent(i_ex[c], w_h.at[oh, pl.ds(c * CR, CR), :])

        @pl.when(depth < 3)
        def _():
            for c in range(NC):
                sent(i_ch[c], w_piece(oseq, c))

        for k in range(3):
            sent(i_wy[k], w_rows(seq))
            for c in range(NC):
                sent(i_wr[c][k], w_piece(oseq, c))

    st_slot = lambda v, h: kvs.at[v, half_rows(h), :]

    def stale_z():
        send(i_sz, st_h.at[oh], st_slot(y, zh), zdev)

    def stale_y():
        for k in range(3):
            send(i_sy[k], st_h.at[zh], st_slot(y, zh), ydev[k])
        local(2, st_h.at[zh], st_slot(y, zh)).start()
        local(3, tx_h.at[zh], tx).start()

    def stale_relay():
        arrived(i_sz, st_slot(y, oh))
        for k in range(3):
            send(i_sr[k], st_slot(y, oh), st_slot(y, oh), ydev[k])

    def stale_all():
        local(2, st_h.at[zh], st_slot(y, zh)).wait()
        local(3, tx_h.at[zh], tx).wait()
        for k in range(3):
            arrived(i_sy[k], st_slot(yfrom[k], zh))
            arrived(i_sr[k], st_slot(yfrom[k], oh))

    def stale_sent():
        sent(i_sz, st_slot(y, zh))
        for k in range(3):
            sent(i_sy[k], st_slot(y, zh))
            sent(i_sr[k], st_slot(y, oh))

    wo_rows = lambda x: wo.at[pl.ds(x * 384, 384), :]

    def out_send():
        for k in range(3):
            send(i_wo[k], wo_h, wo_rows(tp), xdev[k])
        local(4, wo_h, wo_rows(tp)).start()

    def out_all():
        local(4, wo_h, wo_rows(tp)).wait()
        for k in range(3):
            arrived(i_wo[k], wo_rows(xfrom[k]))

    row_id = lax.broadcasted_iota(jnp.int32, (1, 256), 1)
    lane_seg = row_id // 32
    rank_of = [
        [sum(jnp.where(order[s, k] == p, k, 0) for k in range(1, MICRO)) for p in range(MICRO)]
        for s in range(8)
    ]
    col_seg = lax.broadcasted_iota(jnp.int32, (256, 1), 0) // 32
    qrank = jnp.zeros((256, 1), jnp.int32)
    kranks = []
    for v in range(4):
        krank = jnp.zeros((1, 256), jnp.int32)
        for j in range(8):
            scalar = rank_of[(j // 4) * 4 + v][j % 4]
            krank = jnp.where(lane_seg == j, scalar, krank)
            qrank = jnp.where((col_seg == j) & (y == v), scalar, qrank)
        kranks.append(krank)
    low = lax.broadcasted_iota(jnp.int32, (1, 128), 1) < HEAD
    text_live = lax.broadcasted_iota(jnp.int32, (1, 256), 1) < tlen[0]

    def norm_rows(r0, count, shift_ref, scale_ref, store):
        parts = [hx[c, pl.ds(r0, count), :].astype(F32) for c in range(4)]
        total = sum(jnp.sum(part, axis=-1, keepdims=True) for part in parts)
        mean = total * (1.0 / 1536)
        parts = [part - mean for part in parts]
        spread = sum(jnp.sum(part * part, axis=-1, keepdims=True) for part in parts)
        inv = lax.rsqrt(spread * (1.0 / 1536) + 1e-06)
        for c in range(4):
            lanes = slice(c * 384, (c + 1) * 384)
            value = parts[c] * inv * (1.0 + scale_ref(lanes)) + shift_ref(lanes)
            store(c, value.astype(BF16))

    def norm_block(h):
        for b in range(4):
            r0 = h * 128 + b * 32

            def store(c, value, r0=r0):
                nm[c // 2, pl.ds(r0, 32), (c % 2) * 384 : (c % 2) * 384 + 384] = value

            norm_rows(
                r0, 32, lambda l: mod[0:1, l], lambda l: mod[1:2, l], store
            )

    @pl.when(sec == 0)
    def _():
        hidden_send()
        weights_send()

        @pl.when(depth == 3)
        def _():
            hidden_forward()

        weights_relay()

        @pl.when(depth < 3)
        def _():
            hidden_forward()

        hidden_own()
        stale_z()
        stale_y()
        out_send()
        hidden_other()

    @pl.when(sec == 1)
    def _():
        pl.semaphore_wait(go_sem.at[0], 1)
        weights_send()
        stale_z()
        stale_y()
        pl.semaphore_wait(go_sem.at[1], 1)
        out_send()
        weights_relay()
        stale_relay()
        for n in range(4):
            arrived(i_h1[n], hx.at[n])

    norm_block(0)
    norm_block(1)
    weights_near()
    for c in range(5):
        lanes = slice(c * 128, c * 128 + 128)
        acc[:, lanes] = dot(nm[zh], wv[pl.ds(zh * 768, 768), lanes])
    weights_far()
    own = kvf.at[y]
    for c in range(5):
        lanes = slice(c * 128, c * 128 + 128)
        value = (acc[:, lanes] + dot(nm[oh], wv[pl.ds(oh * 768, 768), lanes])).astype(BF16)
        if c < 3:
            kvf[y, :, lanes] = value
        else:
            lhs[:, (c - 3) * 128 : (c - 2) * 128] = value
        if c == 2:
            for k in range(3):
                send(i_kv[k], own, own, ydev[k])
    send(i_nk, kvf.at[y, half_rows(oh), :], nkv, zdev)

    @pl.when(sec == 0)
    def _():
        pl.semaphore_signal(go_sem.at[0], inc=1, device_id=core, device_id_type=MESH)
        stale_relay()

    out_all()

    @pl.when(sec == 0)
    def _():
        pl.semaphore_signal(go_sem.at[1], inc=1, device_id=core, device_id_type=MESH)

    stale_all()
    for k in range(3):
        arrived(i_kv[k], kvf.at[yfrom[k]])

    heads = ((0, 0, 0), (0, 0, 1), (1, 1, 2))
    single_low = zh == 0

    def attend(rb):
        rows = slice(rb * 128, rb * 128 + 128)
        rank = qrank[rows]
        masks = [kranks[v] <= rank for v in range(4)]
        outs = []
        for j in range(3):
            tile = 0 if j < 2 else 1
            query = lhs[rows, tile * 128 : tile * 128 + 128].astype(F32) * (HEAD ** (-0.5))
            if j == 0:
                keep = low
            elif j == 1:
                keep = jnp.logical_not(low)
            else:
                keep = low == single_low
            query = jnp.where(keep, query, 0.0).astype(BF16)
            kl = slice(tile * 128, tile * 128 + 128)
            vl = slice(256, 384) if j < 2 else kl
            for v in range(4):
                fresh = dot_nt(query, kvf[v, :, kl])
                stale = dot_nt(query, kvs[v, :, kl])
                sbuf[:, v * 256 : v * 256 + 256] = jnp.where(masks[v], fresh, stale)
            text = dot_nt(query, tx[:, kl])
            sbuf[:, 1024:1280] = jnp.where(text_live, text, -1e30)
            scores = sbuf[...]
            peak = jnp.max(scores, axis=-1, keepdims=True)
            weights = jnp.exp(scores - peak)
            inv = 1.0 / jnp.sum(weights, axis=-1, keepdims=True)
            sbuf[...] = weights * inv
            total = dot(sbuf[:, 1024:1280].astype(BF16), tx[:, vl])
            for v in range(4):
                weights = sbuf[:, v * 256 : v * 256 + 256]
                fresh = jnp.where(masks[v], weights, 0.0).astype(BF16)
                stale = jnp.where(masks[v], 0.0, weights).astype(BF16)
                total = total + dot(fresh, kvf[v, :, vl]) + dot(stale, kvs[v, :, vl])
            outs.append(total)
        at[zh, tp, rows, :] = jnp.where(low, outs[0], outs[1]).astype(BF16)
        single = jnp.where(low == single_low, 0.0, outs[2])
        return single + pltpu.roll(single, HEAD, 1)

    first = attend(0)
    second = attend(1)
    at[zh, tp, 256:384, :] = jnp.where(low, first, second).astype(BF16)
    mine = at.at[zh, tp]
    send(i_az, mine, mine, zdev)
    for k in range(3):
        send(i_ax[k], mine, mine, xdev[k])

    arrived(i_nk, nkv)
    mine_kv = [kvf[y, half_rows(zh), c * 128 : c * 128 + 128].astype(F32) for c in range(3)]
    their_kv = [nkv[:, c * 128 : c * 128 + 128].astype(F32) for c in range(3)]
    first_kv = [jnp.where(zh == 0, a, b) for a, b in zip(mine_kv, their_kv)]
    second_kv = [jnp.where(zh == 0, b, a) for a, b in zip(mine_kv, their_kv)]
    out_kv[0, :, 0:128] = first_kv[0].astype(BF16)
    out_kv[0, :, 128:256] = jnp.where(low, first_kv[1], second_kv[1]).astype(BF16)
    out_kv[0, :, 256:384] = second_kv[0].astype(BF16)
    out_kv[1, :, 0:128] = first_kv[2].astype(BF16)
    out_kv[1, :, 128:256] = pltpu.roll(
        jnp.where(low, second_kv[1], first_kv[1]), HEAD, 1
    ).astype(BF16)
    out_kv[1, :, 256:384] = second_kv[2].astype(BF16)

    theirs = at.at[oh, tp]
    arrived(i_az, theirs)
    for k in range(3):
        send(i_af[k], theirs, theirs, xdev[k])
    for k in range(3):
        arrived(i_ax[k], at.at[zh, xfrom[k]])
    for k in range(3):
        arrived(i_af[k], at.at[oh, xfrom[k]])
    for x in range(4):
        lhs[:, x * 384 : x * 384 + 128] = at[0, x, 0:256, :]
        lhs[:, x * 384 + 256 : x * 384 + 384] = at[1, x, 0:256, :]
        a = at[0, x, 256:384, :].astype(F32)
        b = at[1, x, 256:384, :].astype(F32)
        tile = slice(x * 384 + 128, x * 384 + 256)
        lhs[0:128, tile] = jnp.where(low, a, pltpu.roll(b, HEAD, 1)).astype(BF16)
        lhs[128:256, tile] = jnp.where(low, pltpu.roll(a, HEAD, 1), b).astype(BF16)

    @pl.when(sec == 0)
    def _():
        hidden_sent()

    for n in range(4):
        lanes = slice(n * 384, n * 384 + 384)
        branch = dot(lhs[...], wo[:, lanes])
        hx[n] = (hx[n].astype(F32) + mod[2:3, lanes] * branch).astype(BF16)

        @pl.when(sec == 0)
        def _(n=n):
            send(i_h1[n], hx.at[n], hx.at[n], core)

    @pl.when(sec == 1)
    def _():
        for b in range(4):
            r0 = zh * 128 + b * 32

            def store(c, value, b=b):
                fin[b * 32 : b * 32 + 32, c * 384 : c * 384 + 384] = value

            norm_rows(r0, 32, lambda l: fmod[0:1, l], lambda l: fmod[1:2, l], store)
        send(i_fn, fin, fin, core)

    @pl.when(sec == 0)
    def _():
        arrived(i_fn, fin)

    out_lat[...] = lat[...] + step[0] * dot(fin[...], wf[...])

    @pl.when(sec == 0)
    def _():
        for n in range(4):
            sent(i_h1[n], hx.at[n])

    @pl.when(sec == 1)
    def _():
        sent(i_fn, fin)

    weights_sent()
    stale_sent()
    for k in range(3):
        sent(i_wo[k], wo_rows(tp))
        sent(i_kv[k], own)
        sent(i_ax[k], mine)
        sent(i_af[k], theirs)
    sent(i_nk, nkv)
    sent(i_az, mine)


def pair_of(block, half):
    return block[..., 0:128] if half == 0 else block[..., 256:384]


def kv_tiles(k, v, half):
    if half == 0:
        single = [k[..., 128:192], v[..., 128:192]]
    else:
        single = [v[..., 192:256], k[..., 192:256]]
    return [pair_of(k, half)] + single + [pair_of(v, half)]


def body(
    hidden, latent, w_qkv, w_out, modulation, final_mod, w_final, stale_kv, text_kv, text_len,
    patch_order, step_size,
):
    w = w_qkv[0]
    q, k, v = w[:, 0], w[:, 1], w[:, 2]
    weights = jnp.stack(
        [
            jnp.concatenate(kv_tiles(k, v, h) + [pair_of(q, h), q[:, 128:256]], axis=-1)
            for h in range(2)
        ]
    )
    stale = jnp.stack(
        [jnp.concatenate(kv_tiles(stale_kv[0, 0], stale_kv[0, 1], h), axis=-1) for h in range(2)]
    )
    text = jnp.stack(
        [jnp.concatenate(kv_tiles(text_kv[0, 0], text_kv[0, 1], h), axis=-1) for h in range(2)]
    )
    text = jnp.pad(text, ((0, 0), (0, 256 - text.shape[1]), (0, 0)))
    smem = pl.BlockSpec(memory_space=pltpu.SMEM)
    vmem = pl.BlockSpec(memory_space=pltpu.VMEM)
    any_ = pl.BlockSpec(memory_space=pl.ANY)
    lat_next, kv_next = pl.pallas_call(
        kernel,
        out_shape=(
            jax.ShapeDtypeStruct((128, 8), F32),
            jax.ShapeDtypeStruct((2, 128, 384), BF16),
        ),
        in_specs=[smem, smem, smem, any_, any_, any_, any_, any_, vmem, vmem, vmem, vmem],
        out_specs=(vmem, vmem),
        scratch_shapes=[
            pltpu.VMEM((4, 256, 384), BF16),
            pltpu.VMEM((1536, 640), BF16),
            pltpu.VMEM((4, 256, 384), BF16),
            pltpu.VMEM((4, 256, 384), BF16),
            pltpu.VMEM((256, 384), BF16),
            pltpu.VMEM((1536, 1536), BF16),
            pltpu.VMEM((2, 256, 768), BF16),
            pltpu.VMEM((2, 4, 384, 128), BF16),
            pltpu.VMEM((256, 1536), BF16),
            pltpu.VMEM((128, 384), BF16),
            pltpu.VMEM((128, 1536), BF16),
            pltpu.VMEM((256, 640), F32),
            pltpu.VMEM((128, 1280), F32),
            pltpu.SemaphoreType.DMA((N_LINK,)),
            pltpu.SemaphoreType.DMA((N_LINK,)),
            pltpu.SemaphoreType.DMA((N_LOCAL,)),
            pltpu.SemaphoreType.REGULAR((2,)),
        ],
        compiler_params=pltpu.CompilerParams(
            collective_id=0, has_side_effects=True, vmem_limit_bytes=48 << 20
        ),
        name="both_layers",
    )(
        patch_order, text_len, step_size, hidden, weights, w_out[0], stale, text, modulation[0],
        final_mod, w_final, latent,
    )
    return lat_next, kv_next[None]


def solution(mesh):
    return jax.shard_map(
        body,
        mesh=mesh,
        in_specs=(
            P(("req", "seq"), "tp"),
            P(("req", "seq"), ("section", "tp")),
            P("section", "seq", None, "tp"),
            P("section", "tp", None),
            P("section", None, None),
            P(),
            P(None, ("section", "tp")),
            P("section", None, ("req", "seq"), "tp"),
            P("section", None, "req", "tp"),
            P("req"),
            P("req", None),
            P(),
        ),
        out_specs=(P(("req", "seq"), ("section", "tp")), P("section", None, ("req", "seq"), "tp")),
        check_vma=False,
    )
```

```python
import jax
import jax.numpy as jnp
from jax import lax
from jax.experimental import pallas as pl
from jax.experimental.pallas import tpu as pltpu
from jax.sharding import PartitionSpec as P

HEAD = 64
MICRO = 4
NC = 4
MESH = pl.DeviceIdType.MESH
F32 = jnp.float32
BF16 = jnp.bfloat16


def dot(a, b):
    return jnp.dot(a, b, preferred_element_type=F32)


def dot_nt(a, b):
    return lax.dot_general(a, b, (((1,), (1,)), ((), ())), preferred_element_type=F32)


class Link:
    def __init__(self, send_sem, recv_sem):
        self.send_sem, self.recv_sem, self.used = send_sem, recv_sem, 0

    def take(self):
        index = self.used
        self.used += 1
        return index

    def make(self, index, src, dst, device):
        return pltpu.make_async_remote_copy(
            src_ref=src,
            dst_ref=dst,
            send_sem=self.send_sem.at[index],
            recv_sem=self.recv_sem.at[index],
            device_id=device,
            device_id_type=MESH,
        )


N_LINK = 72
N_LOCAL = 12


def kernel(
    order_h, tlen_h, step_h, hid_h, wq_h, wo_h, st_h, tx_h, mod_h, fmod_h, wf_h, lat_h,
    out_lat, out_kv,
    hx, wraw, wex, wv, kvf, kvs, straw, sex, txraw, tx, wo, nm, at, lhs, nkv, fin, acc, sbuf,
    mod, fmod, wf, lat, order, tlen, step,
    send_sem, recv_sem, loc_sem, go_sem,
):
    sec = lax.axis_index("section")
    seq = lax.axis_index("seq")
    tp = lax.axis_index("tp")
    req = lax.axis_index("req")
    zh = seq // 4
    oh = 1 - zh
    y = seq % 4
    z = zh * 8 + req
    far = req // 4
    hop = 1 - 2 * far
    depth = req + far * (7 - 2 * req)
    xs = [(tp + k) % 4 for k in (1, 2, 3)]
    ys = [(y + k) % 4 for k in (1, 2, 3)]
    xfrom = [(tp + 4 - k) % 4 for k in (1, 2, 3)]
    yfrom = [(y + 4 - k) % 4 for k in (1, 2, 3)]
    xdev = [{"tp": v} for v in xs]
    ydev = [{"seq": zh * 4 + v} for v in ys]
    zdev = {"seq": (seq + 4) % 8}
    core = {"section": 1 - sec}

    def along_z(steps):
        place = (z + steps + 16) % 16
        return {"seq": (place // 8) * 4 + y, "req": place % 8}

    next_dev = along_z(hop)
    prev_dev = along_z(-hop)
    over_dev = along_z(-4 * hop)

    barrier = pltpu.get_barrier_semaphore()
    for device in xdev + ydev + [zdev, core, next_dev, prev_dev, over_dev]:
        pl.semaphore_signal(barrier, inc=1, device_id=device, device_id_type=MESH)

    link = Link(send_sem, recv_sem)
    half_rows = lambda h: pl.ds(h * 128, 128)
    three = range(3)
    i_hx = [link.take() for _ in three]
    i_hz = link.take()
    i_hf = [link.take() for _ in three]
    i_wy = [link.take() for _ in three]
    i_ch = [link.take() for _ in range(NC)]
    i_ex = [link.take() for _ in range(NC)]
    i_wr = [[link.take() for _ in three] for _ in range(NC)]
    i_sy = [link.take() for _ in three]
    i_sz = link.take()
    i_sr = [link.take() for _ in three]
    i_wo = [[link.take() for _ in three] for _ in range(2)]
    i_kv = [link.take() for _ in three]
    i_nk = link.take()
    i_ax = [[link.take() for _ in three] for _ in range(2)]
    i_az = [link.take() for _ in range(2)]
    i_af = [[link.take() for _ in three] for _ in range(2)]
    i_h1 = [[link.take() for _ in range(4)] for _ in range(2)]
    i_fn = link.take()

    def send(index, src, dst, device):
        link.make(index, src, dst, device).start()

    def arrived(index, dst):
        link.make(index, dst, dst, core).wait_recv()

    def sent(index, src):
        link.make(index, src, src, core).wait_send()

    hx_slot = lambda x, h: hx.at[x, half_rows(h), :]

    wo_rows = lambda x, part: wo.at[pl.ds(x * 384 + part * 192, 192), :]
    local = [
        pltpu.make_async_copy(src, dst, loc_sem.at[n])
        for n, (src, dst) in enumerate(
            [
                (wq_h, wraw),
                (hid_h, hx_slot(tp, zh)),
                (st_h, straw),
                (tx_h, txraw),
                (mod_h, mod),
                (order_h, order),
                (tlen_h, tlen),
                (step_h, step),
                (fmod_h, fmod),
                (wf_h, wf),
                (lat_h, lat),
                (wo_h, wo.at[pl.ds(tp * 384, 384), :]),
            ]
        )
    ]
    local[0].start()

    @pl.when(sec == 0)
    def _():
        local[1].start()

    for copy in local[2:]:
        copy.start()

    low = lax.broadcasted_iota(jnp.int32, (1, 128), 1) < HEAD
    single_low = zh == 0
    tiles = [slice(c * 128, c * 128 + 128) for c in range(12)]

    def turn(value):
        return pltpu.roll(value.astype(F32), HEAD, 1)

    def both_singles(k_tile, v_tile):
        turned = turn(v_tile)
        k_tile = k_tile.astype(F32)
        zero = jnp.where(low, k_tile, turned).astype(BF16)
        one = jnp.where(low, turned, k_tile).astype(BF16)
        return jnp.where(single_low, zero, one), jnp.where(single_low, one, zero)

    def both_pairs(first, last):
        return jnp.where(single_low, first, last), jnp.where(single_low, last, first)

    CR = 192 // NC
    w_rows = lambda s: wv.at[pl.ds(s * 192, 192), :]
    w_piece = lambda s, c: wv.at[pl.ds(s * 192 + c * CR, CR), :]
    x_piece = lambda c: wex.at[pl.ds(c * CR, CR), :]

    def put_w(tile, values):
        wv[pl.ds(seq * 192, 192), tiles[tile]] = values[0]
        wex[:, tiles[tile]] = values[1]

    local[0].wait()
    put_w(0, both_pairs(wraw[1, :, tiles[0]], wraw[1, :, tiles[2]]))
    put_w(1, both_singles(wraw[1, :, tiles[1]], wraw[2, :, tiles[1]]))
    put_w(2, both_pairs(wraw[2, :, tiles[0]], wraw[2, :, tiles[2]]))
    put_w(3, both_pairs(wraw[0, :, tiles[0]], wraw[0, :, tiles[2]]))
    put_w(4, [wraw[0, :, tiles[1]]] * 2)

    pl.semaphore_wait(barrier, 11)

    def hidden_send():
        send(i_hz, hid_h, hx_slot(tp, zh), zdev)
        for k in three:
            send(i_hx[k], hid_h, hx_slot(tp, zh), xdev[k])

    def hidden_own():
        local[1].wait()
        for k in three:
            arrived(i_hx[k], hx_slot(xfrom[k], zh))

    def hidden_forward():
        arrived(i_hz, hx_slot(tp, oh))
        for k in three:
            send(i_hf[k], hx_slot(tp, oh), hx_slot(tp, oh), xdev[k])

    def hidden_other():
        for k in three:
            arrived(i_hf[k], hx_slot(xfrom[k], oh))

    def hidden_sent():
        sent(i_hz, hid_h)
        for k in three:
            sent(i_hx[k], hid_h)
            sent(i_hf[k], hx_slot(tp, oh))


    def weights_cross():
        for at_depth, device in ((0, prev_dev), (1, over_dev)):

            @pl.when(depth == at_depth)
            def _(device=device):
                for c in range(NC):
                    pltpu.make_async_remote_copy(
                        src_ref=x_piece(c),
                        dst_ref=w_piece(seq, c),
                        send_sem=send_sem.at[i_ex[c]],
                        recv_sem=recv_sem.at[i_ch[c]],
                        device_id=device,
                        device_id_type=MESH,
                    ).start()

    def weights_y():
        for k in three:
            send(i_wy[k], w_rows(seq), w_rows(seq), ydev[k])

    oseq = oh * 4 + y

    def weights_pass(c):
        arrived(i_ch[c], w_piece(oseq, c))

        @pl.when(depth % 2 == 0)
        def _():
            send(i_ch[c], w_piece(oseq, c), w_piece(oseq, c), next_dev)

    def weights_relay(c):
        for k in three:
            send(i_wr[c][k], w_piece(oseq, c), w_piece(oseq, c), ydev[k])

    def weights_near():
        for k in three:
            arrived(i_wy[k], w_rows(zh * 4 + yfrom[k]))

    def weights_far():
        for c in range(NC):
            for k in three:
                arrived(i_wr[c][k], w_piece(oh * 4 + yfrom[k], c))

    def weights_sent():
        @pl.when(depth < 2)
        def _():
            for c in range(NC):
                sent(i_ex[c], x_piece(c))

        @pl.when(depth % 2 == 0)
        def _():
            for c in range(NC):
                sent(i_ch[c], w_piece(oseq, c))

        for k in three:
            sent(i_wy[k], w_rows(seq))
            for c in range(NC):
                sent(i_wr[c][k], w_piece(oseq, c))

    st_slot = lambda v, h: kvs.at[v, half_rows(h), :]

    def stale_tiles():
        local[2].wait()

        def put(tile, values):
            kvs[y, half_rows(zh), tiles[tile]] = values[0]
            sex[:, tiles[tile]] = values[1]

        put(0, both_pairs(straw[0, :, tiles[0]], straw[0, :, tiles[2]]))
        put(1, both_singles(straw[0, :, tiles[1]], straw[1, :, tiles[1]]))
        put(2, both_pairs(straw[1, :, tiles[0]], straw[1, :, tiles[2]]))

    def text_tiles():
        local[3].wait()
        tx[144:256, :] = jnp.zeros((112, 384), BF16)
        live = slice(0, txraw.shape[1])
        tx[live, tiles[0]] = both_pairs(txraw[0, :, tiles[0]], txraw[0, :, tiles[2]])[0]
        tx[live, tiles[1]] = both_singles(txraw[0, :, tiles[1]], txraw[1, :, tiles[1]])[0]
        tx[live, tiles[2]] = both_pairs(txraw[1, :, tiles[0]], txraw[1, :, tiles[2]])[0]

    def stale_z():
        send(i_sz, sex, st_slot(y, zh), zdev)

    def stale_y():
        for k in three:
            send(i_sy[k], st_slot(y, zh), st_slot(y, zh), ydev[k])

    def stale_relay():
        arrived(i_sz, st_slot(y, oh))
        for k in three:
            send(i_sr[k], st_slot(y, oh), st_slot(y, oh), ydev[k])

    def stale_all():
        for k in three:
            arrived(i_sy[k], st_slot(yfrom[k], zh))
            arrived(i_sr[k], st_slot(yfrom[k], oh))

    def stale_sent():
        sent(i_sz, sex)
        for k in three:
            sent(i_sy[k], st_slot(y, zh))
            sent(i_sr[k], st_slot(y, oh))

    def out_send(part):
        for k in three:
            send(i_wo[part][k], wo_h.at[pl.ds(part * 192, 192), :], wo_rows(tp, part), xdev[k])

    def out_all():
        local[11].wait()
        for k in three:
            for part in range(2):
                arrived(i_wo[part][k], wo_rows(xfrom[k], part))

    def norm_rows(r0, count, shift, scale, store):
        parts = [hx[c, pl.ds(r0, count), :].astype(F32) for c in range(4)]
        total = sum(jnp.sum(part, axis=-1, keepdims=True) for part in parts)
        mean = total * (1.0 / 1536)
        parts = [part - mean for part in parts]
        spread = sum(jnp.sum(part * part, axis=-1, keepdims=True) for part in parts)
        inv = lax.rsqrt(spread * (1.0 / 1536) + 1e-06)
        for c in range(4):
            lanes = slice(c * 384, (c + 1) * 384)
            store(c, (parts[c] * inv * (1.0 + scale(lanes)) + shift(lanes)).astype(BF16))

    def norm_block(h):
        for b in range(4):
            r0 = h * 128 + b * 32

            def store(c, value, r0=r0):
                nm[c // 2, pl.ds(r0, 32), (c % 2) * 384 : (c % 2) * 384 + 384] = value

            norm_rows(r0, 32, lambda l: mod[0, :, l], lambda l: mod[1, :, l], store)

    def go(index):
        pl.semaphore_signal(go_sem.at[index], inc=1, device_id=core, device_id_type=MESH)

    def go_wait(index):
        pl.semaphore_wait(go_sem.at[index], 1)

    @pl.when(sec == 0)
    def _():
        hidden_send()
        weights_cross()
        weights_y()

    @pl.when(sec == 1)
    def _():
        out_send(0)

    stale_tiles()
    for copy in local[4:11]:
        copy.wait()

    @pl.when(sec == 0)
    def _():
        @pl.when(depth == 3)
        def _():
            hidden_forward()

        for c in range(NC):
            weights_pass(c)
            weights_relay(c)

        @pl.when(depth < 3)
        def _():
            hidden_forward()

        stale_z()
        out_send(0)
        out_send(1)
        go(0)
        stale_y()
        hidden_own()
        norm_block(zh)
        text_tiles()
        hidden_other()
        norm_block(oh)

    @pl.when(sec == 1)
    def _():
        text_tiles()
        go_wait(0)
        stale_z()
        weights_cross()
        for c in range(NC):
            weights_pass(c)
        go_wait(1)
        weights_y()
        for c in range(NC):
            weights_relay(c)
        stale_y()
        stale_relay()
        go_wait(2)
        out_send(1)
        for n in range(4):
            arrived(i_h1[0][n], hx.at[n, half_rows(zh), :])
        norm_block(zh)
        for n in range(4):
            arrived(i_h1[1][n], hx.at[n, half_rows(oh), :])
        norm_block(oh)

    segment = lax.broadcasted_iota(jnp.int32, (1, 256), 1) // 32
    rank_of = [
        [sum(jnp.where(order[k, s] == p, k, 0) for k in range(1, MICRO)) for p in range(MICRO)]
        for s in range(8)
    ]
    row_segment = lax.broadcasted_iota(jnp.int32, (256, 1), 0) // 32
    qrank = jnp.zeros((256, 1), jnp.int32)
    kranks = []
    for v in range(4):
        krank = jnp.zeros((1, 256), jnp.int32)
        for j in range(8):
            scalar = rank_of[(j // 4) * 4 + v][j % 4]
            krank = jnp.where(segment == j, scalar, krank)
            qrank = jnp.where((row_segment == j) & (y == v), scalar, qrank)
        kranks.append(krank)
    text_live = lax.broadcasted_iota(jnp.int32, (1, 256), 1) < tlen[0]

    weights_near()
    for c in range(5):
        acc[:, tiles[c]] = dot(nm[zh], wv[pl.ds(zh * 768, 768), tiles[c]])
    weights_far()
    own = kvf.at[y]
    for c in range(5):
        value = acc[:, tiles[c]] + dot(nm[oh], wv[pl.ds(oh * 768, 768), tiles[c]])
        if c < 3:
            kvf[y, :, tiles[c]] = value.astype(BF16)
        else:
            lhs[:, tiles[c - 3]] = value.astype(BF16)
        if c == 2:
            for k in three:
                send(i_kv[k], own, own, ydev[k])
    send(i_nk, kvf.at[y, half_rows(oh), :], nkv, zdev)

    @pl.when(sec == 0)
    def _():
        stale_relay()

    stale_all()
    for k in three:
        arrived(i_kv[k], kvf.at[yfrom[k]])

    @pl.when(sec == 0)
    def _():
        go(1)

    def attend(rb):
        rows = half_rows(rb)
        rank = jnp.where(rb == 0, qrank[0:128], qrank[128:256])
        masks = [kranks[v] <= rank for v in range(4)]
        outs = []
        for j in range(3):
            tile = 0 if j < 2 else 1
            query = lhs[rows, tiles[tile]].astype(F32) * (HEAD ** (-0.5))
            if j == 0:
                keep = low
            elif j == 1:
                keep = jnp.logical_not(low)
            else:
                keep = low == single_low
            query = jnp.where(keep, query, 0.0).astype(BF16)
            kl = tiles[tile]
            vl = tiles[2] if j < 2 else kl
            for v in range(4):
                fresh = dot_nt(query, kvf[v, :, kl])
                stale = dot_nt(query, kvs[v, :, kl])
                sbuf[:, v * 256 : v * 256 + 256] = jnp.where(masks[v], fresh, stale)
            text = dot_nt(query, tx[:, kl])
            sbuf[:, 1024:1280] = jnp.where(text_live, text, -1e30)
            scores = sbuf[...]
            peak = jnp.max(scores, axis=-1, keepdims=True)
            weights = jnp.exp(scores - peak)
            inv = 1.0 / jnp.sum(weights, axis=-1, keepdims=True)
            sbuf[...] = weights * inv
            total = dot(sbuf[:, 1024:1280].astype(BF16), tx[:, vl])
            for v in range(4):
                weights = sbuf[:, v * 256 : v * 256 + 256]
                fresh = jnp.where(masks[v], weights, 0.0).astype(BF16)
                stale = jnp.where(masks[v], 0.0, weights).astype(BF16)
                total = total + dot(fresh, kvf[v, :, vl]) + dot(stale, kvs[v, :, vl])
            outs.append(total)
        at[zh, tp, rb, 0:128, :] = jnp.where(low, outs[0], outs[1]).astype(BF16)
        single = jnp.where(low == single_low, 0.0, outs[2])
        single = single + pltpu.roll(single, HEAD, 1)
        at[zh, tp, rb, 128:192, :] = jnp.where(low, single[0:64], single[64:128]).astype(BF16)

    block = lambda a, x, rb: at.at[a, x, rb]
    attend(oh)
    send(i_az[0], block(zh, tp, oh), block(zh, tp, oh), zdev)

    @pl.when(sec == 0)
    def _():
        for k in three:
            send(i_ax[1][k], block(zh, tp, oh), block(zh, tp, oh), xdev[k])

    attend(zh)

    @pl.when(sec == 0)
    def _():
        send(i_az[1], block(zh, tp, zh), block(zh, tp, zh), zdev)

    for k in three:
        send(i_ax[0][k], block(zh, tp, zh), block(zh, tp, zh), xdev[k])

    arrived(i_nk, nkv)
    mine_kv = [kvf[y, half_rows(zh), tiles[c]] for c in range(3)]
    their_kv = [nkv[:, tiles[c]] for c in range(3)]
    first_kv = [jnp.where(single_low, a, b) for a, b in zip(mine_kv, their_kv)]
    second_kv = [jnp.where(single_low, b, a) for a, b in zip(mine_kv, their_kv)]
    out_kv[0, :, tiles[0]] = first_kv[0]
    out_kv[0, :, tiles[1]] = jnp.where(low, first_kv[1], second_kv[1])
    out_kv[0, :, tiles[2]] = second_kv[0]
    out_kv[1, :, tiles[0]] = first_kv[2]
    out_kv[1, :, tiles[1]] = turn(jnp.where(low, second_kv[1], first_kv[1])).astype(BF16)
    out_kv[1, :, tiles[2]] = second_kv[2]

    arrived(i_az[0], block(oh, tp, zh))
    for k in three:
        send(i_af[0][k], block(oh, tp, zh), block(oh, tp, zh), xdev[k])

    @pl.when(sec == 0)
    def _():
        arrived(i_az[1], block(oh, tp, oh))
        for k in three:
            send(i_af[1][k], block(oh, tp, oh), block(oh, tp, oh), xdev[k])
        hidden_sent()

    def out_rows(part, rb):
        for k in three:
            arrived(i_ax[part][k], block(zh, xfrom[k], rb))
        for k in three:
            arrived(i_af[part][k], block(oh, xfrom[k], rb))
        for x in range(4):
            lhs[0:128, tiles[3 * x]] = at[0, x, rb, 0:128, :]
            lhs[0:128, tiles[3 * x + 2]] = at[1, x, rb, 0:128, :]
            a = at[0, x, rb, 128:192, :]
            b = at[1, x, rb, 128:192, :]
            lhs[0:64, tiles[3 * x + 1]] = jnp.where(low, a.astype(F32), turn(b)).astype(BF16)
            lhs[64:128, tiles[3 * x + 1]] = jnp.where(low, turn(a), b.astype(F32)).astype(BF16)
        for n in range(4):
            lanes = slice(n * 384, n * 384 + 384)
            branch = dot(lhs[0:128, :], wo[:, lanes])
            rows = half_rows(rb)
            hx[n, rows, :] = (hx[n, rows, :].astype(F32) + mod[2, :, lanes] * branch).astype(BF16)

            @pl.when(sec == 0)
            def _():
                send(i_h1[part][n], hx.at[n, rows, :], hx.at[n, rows, :], core)

    out_all()
    out_rows(0, zh)

    @pl.when(sec == 0)
    def _():
        out_rows(1, oh)
        go(2)

    @pl.when(sec == 1)
    def _():
        for b in range(4):

            def store(c, value, b=b):
                fin[b * 32 : b * 32 + 32, c * 384 : c * 384 + 384] = value

            norm_rows(
                zh * 128 + b * 32, 32, lambda l: fmod[0:1, l], lambda l: fmod[1:2, l], store
            )
        send(i_fn, fin, fin, core)

    @pl.when(sec == 0)
    def _():
        arrived(i_fn, fin)

    out_lat[...] = lat[...] + step[0] * dot_nt(wf[...], fin[...])

    @pl.when(sec == 0)
    def _():
        for part, rb in ((0, zh), (1, oh)):
            for n in range(4):
                sent(i_h1[part][n], hx.at[n, half_rows(rb), :])
        sent(i_az[1], block(zh, tp, zh))
        for k in three:
            sent(i_ax[1][k], block(zh, tp, oh))
            sent(i_af[1][k], block(oh, tp, oh))

    @pl.when(sec == 1)
    def _():
        sent(i_fn, fin)

    weights_sent()
    stale_sent()
    for k in three:
        for part in range(2):
            sent(i_wo[part][k], wo_rows(tp, part))
        sent(i_kv[k], own)
        sent(i_ax[0][k], block(zh, tp, zh))
        sent(i_af[0][k], block(oh, tp, zh))
    sent(i_nk, nkv)
    sent(i_az[0], block(zh, tp, oh))


def body(
    hidden, latent, w_qkv, w_out, modulation, final_mod, w_final, stale_kv, text_kv, text_len,
    patch_order, step_size,
):
    vmem = pl.BlockSpec(memory_space=pltpu.VMEM)
    any_ = pl.BlockSpec(memory_space=pltpu.HBM)
    text = text_kv[0]
    lat_next, kv_next = pl.pallas_call(
        kernel,
        out_shape=(
            jax.ShapeDtypeStruct((8, 128), F32),
            jax.ShapeDtypeStruct((2, 128, 384), BF16),
        ),
        in_specs=[any_] * 12,
        out_specs=(vmem, vmem),
        scratch_shapes=[
            pltpu.VMEM((4, 256, 384), BF16),
            pltpu.VMEM((3, 192, 384), BF16),
            pltpu.VMEM((192, 640), BF16),
            pltpu.VMEM((1536, 640), BF16),
            pltpu.VMEM((4, 256, 384), BF16),
            pltpu.VMEM((4, 256, 384), BF16),
            pltpu.VMEM((2, 128, 384), BF16),
            pltpu.VMEM((128, 384), BF16),
            pltpu.VMEM(text.shape, BF16),
            pltpu.VMEM((256, 384), BF16),
            pltpu.VMEM((1536, 1536), BF16),
            pltpu.VMEM((2, 256, 768), BF16),
            pltpu.VMEM((2, 4, 2, 192, 128), BF16),
            pltpu.VMEM((256, 1536), BF16),
            pltpu.VMEM((128, 384), BF16),
            pltpu.VMEM((128, 1536), BF16),
            pltpu.VMEM((256, 640), F32),
            pltpu.VMEM((128, 1280), F32),
            pltpu.VMEM((3, 1, 1536), F32),
            pltpu.VMEM((2, 1536), F32),
            pltpu.VMEM((8, 1536), BF16),
            pltpu.VMEM((8, 128), F32),
            pltpu.SMEM((4, 8), jnp.int32),
            pltpu.SMEM((1,), jnp.int32),
            pltpu.SMEM((1,), F32),
            pltpu.SemaphoreType.DMA((N_LINK,)),
            pltpu.SemaphoreType.DMA((N_LINK,)),
            pltpu.SemaphoreType.DMA((N_LOCAL,)),
            pltpu.SemaphoreType.REGULAR((3,)),
        ],
        compiler_params=pltpu.CompilerParams(
            collective_id=0, has_side_effects=True, vmem_limit_bytes=63 << 20
        ),
        name="both_layers",
    )(
        patch_order.T, text_len, step_size, hidden, w_qkv[0].transpose(1, 0, 2), w_out[0],
        stale_kv[0], text, modulation.transpose(1, 0, 2), final_mod, w_final.T, latent.T,
    )
    return lat_next.T, kv_next[None]


def solution(mesh):
    return jax.shard_map(
        body,
        mesh=mesh,
        in_specs=(
            P(("req", "seq"), "tp"),
            P(("req", "seq"), ("section", "tp")),
            P("section", "seq", None, "tp"),
            P("section", "tp", None),
            P("section", None, None),
            P(),
            P(None, ("section", "tp")),
            P("section", None, ("req", "seq"), "tp"),
            P("section", None, "req", "tp"),
            P("req"),
            P("req", None),
            P(),
        ),
        out_specs=(P(("req", "seq"), ("section", "tp")), P("section", None, ("req", "seq"), "tp")),
        check_vma=False,
    )
```

```python
import jax
import jax.numpy as jnp
from jax import lax
from jax.experimental import pallas as pl
from jax.experimental.pallas import tpu as pltpu
from jax.sharding import PartitionSpec as P

HEAD = 64
MICRO = 4
NC = 5
HC = 2
MESH = pl.DeviceIdType.MESH
F32 = jnp.float32
BF16 = jnp.bfloat16


def dot(a, b):
    return jnp.dot(a, b, preferred_element_type=F32)


def dot_nt(a, b):
    return lax.dot_general(a, b, (((1,), (1,)), ((), ())), preferred_element_type=F32)


class Link:
    def __init__(self, send_sem, recv_sem):
        self.send_sem, self.recv_sem, self.used = send_sem, recv_sem, 0

    def take(self):
        index = self.used
        self.used += 1
        return index

    def make(self, index, src, dst, device):
        return pltpu.make_async_remote_copy(
            src_ref=src,
            dst_ref=dst,
            send_sem=self.send_sem.at[index],
            recv_sem=self.recv_sem.at[index],
            device_id=device,
            device_id_type=MESH,
        )


N_LINK = 112
N_LOCAL = 12


def kernel(
    order_h, tlen_h, step_h, hid_h, wq_h, wo_h, st_h, tx_h, mod_h, fmod_h, wf_h, lat_h,
    out_lat, out_kv,
    hx, hland, wraw, wex, wv, kvf, kvs, straw, sex, txraw, tx, wo, nm, at, lhs, nkv, fin, acc, sbuf,
    mod, fmod, wf, vel, lat, order, tlen, step,
    send_sem, recv_sem, loc_sem, go_sem,
):
    sec = lax.axis_index("section")
    seq = lax.axis_index("seq")
    tp = lax.axis_index("tp")
    req = lax.axis_index("req")
    zh = seq // 4
    oh = 1 - zh
    y = seq % 4
    z = zh * 8 + req
    far = req // 4
    hop = 1 - 2 * far
    depth = req + far * (7 - 2 * req)
    xs = [(tp + k) % 4 for k in (1, 2, 3)]
    ys = [(y + k) % 4 for k in (1, 2, 3)]
    xfrom = [(tp + 4 - k) % 4 for k in (1, 2, 3)]
    yfrom = [(y + 4 - k) % 4 for k in (1, 2, 3)]
    xdev = [{"tp": v} for v in xs]
    ydev = [{"seq": zh * 4 + v} for v in ys]
    zdev = {"seq": (seq + 4) % 8}
    core = {"section": 1 - sec}
    xcross = [{"tp": v, "section": 1 - sec} for v in xs]

    def along_z(steps):
        place = (z + steps + 16) % 16
        return {"seq": (place // 8) * 4 + y, "req": place % 8}

    cross_dev = along_z(-2 * hop)
    pass_dev = [along_z(hop), along_z(2 * hop), along_z(-hop)]

    barrier = pltpu.get_barrier_semaphore()
    for device in xdev + xcross + ydev + [zdev, core, cross_dev] + pass_dev:
        pl.semaphore_signal(barrier, inc=1, device_id=device, device_id_type=MESH)

    link = Link(send_sem, recv_sem)
    half_rows = lambda h: pl.ds(h * 128, 128)
    three = range(3)
    i_hx = [link.take() for _ in three]
    i_hz = [link.take() for _ in range(HC)]
    i_hf = [[link.take() for _ in range(4)] for _ in range(HC)]
    i_wy = [link.take() for _ in three]
    i_ch = [link.take() for _ in range(NC)]
    i_ex = [link.take() for _ in range(NC)]
    i_ps = [[link.take() for _ in three] for _ in range(NC)]
    i_wr = [[link.take() for _ in three] for _ in range(NC)]
    i_sy = [link.take() for _ in three]
    i_sz = link.take()
    i_sr = [link.take() for _ in three]
    i_wo = [[link.take() for _ in three] for _ in range(2)]
    i_kv = [[link.take() for _ in three] for _ in range(3)]
    i_nk = link.take()
    i_ax = [[link.take() for _ in three] for _ in range(2)]
    i_az = [link.take() for _ in range(2)]
    i_af = [[link.take() for _ in three] for _ in range(2)]
    i_h1 = [[link.take() for _ in range(4)] for _ in range(2)]
    i_fn = link.take()
    i_wf = link.take()

    def send(index, src, dst, device):
        link.make(index, src, dst, device).start()

    def arrived(index, dst):
        link.make(index, dst, dst, core).wait_recv()

    def sent(index, src):
        link.make(index, src, src, core).wait_send()

    hx_slot = lambda x, h: hx.at[x, half_rows(h), :]

    wo_part = lambda start, part: pl.ds(start + part * 96, (96, 288)[part])
    wo_rows = lambda x, part: wo.at[wo_part(x * 384, part), :]
    local = [
        pltpu.make_async_copy(src, dst, loc_sem.at[n])
        for n, (src, dst) in enumerate(
            [
                (wq_h, wraw),
                (hid_h, hx_slot(tp, zh)),
                (st_h, straw),
                (tx_h, txraw),
                (mod_h, mod),
                (order_h, order),
                (tlen_h, tlen),
                (step_h, step),
                (fmod_h, fmod),
                (wf_h, wf.at[0]),
                (lat_h, lat),
                (wo_h, wo.at[pl.ds(tp * 384, 384), :]),
            ]
        )
    ]
    local[0].start()

    @pl.when(sec == 0)
    def _():
        local[1].start()

    for copy in local[2:]:
        copy.start()

    low = lax.broadcasted_iota(jnp.int32, (1, 128), 1) < HEAD
    single_low = zh == 0
    tiles = [slice(c * 128, c * 128 + 128) for c in range(12)]

    def turn(value):
        return pltpu.roll(value.astype(F32), HEAD, 1)

    def both_singles(k_tile, v_tile):
        turned = turn(v_tile)
        k_tile = k_tile.astype(F32)
        zero = jnp.where(low, k_tile, turned).astype(BF16)
        one = jnp.where(low, turned, k_tile).astype(BF16)
        return jnp.where(single_low, zero, one), jnp.where(single_low, one, zero)

    def both_pairs(first, last):
        return jnp.where(single_low, first, last), jnp.where(single_low, last, first)

    w_rows = lambda s: wv.at[:, pl.ds(s * 192, 192), :]
    w_piece = lambda s, c: wv.at[c, pl.ds(s * 192, 192), :]
    x_piece = lambda c: wex.at[c]

    def put_w(tile, values):
        wv[tile, pl.ds(seq * 192, 192), :] = values[0]
        wex[tile] = values[1]

    local[0].wait()
    put_w(0, both_pairs(wraw[1, :, tiles[0]], wraw[1, :, tiles[2]]))
    put_w(1, both_singles(wraw[1, :, tiles[1]], wraw[2, :, tiles[1]]))
    put_w(2, both_pairs(wraw[2, :, tiles[0]], wraw[2, :, tiles[2]]))
    put_w(3, both_pairs(wraw[0, :, tiles[0]], wraw[0, :, tiles[2]]))
    put_w(4, [wraw[0, :, tiles[1]]] * 2)

    pl.semaphore_wait(barrier, 15)

    HR = 128 // HC
    h_piece = lambda c: pl.ds(c * HR, HR)
    h_slot = lambda x, h, c: hx.at[x, pl.ds(h * 128 + c * HR, HR), :]

    def hidden_send():
        for k in three:
            send(i_hx[k], hid_h, hx_slot(tp, zh), xdev[k])

    def hidden_own():
        local[1].wait()
        for k in three:
            arrived(i_hx[k], hx_slot(xfrom[k], zh))

    def hidden_cross():
        for c in range(HC):
            send(i_hz[c], hid_h.at[h_piece(c), :], hland.at[h_piece(c), :], zdev)

    def hidden_forward():
        for c in range(HC):
            arrived(i_hz[c], hland.at[h_piece(c), :])
            for k, device in enumerate(xcross + [core]):
                send(i_hf[c][k], hland.at[h_piece(c), :], h_slot(tp, oh, c), device)

    def hidden_other():
        for c in range(HC):
            for k in range(4):
                arrived(i_hf[c][k], h_slot((xfrom + [tp])[k], oh, c))

    def hidden_sent():
        for c in range(HC):
            sent(i_hz[c], hid_h.at[h_piece(c), :])
            for k in range(4):
                sent(i_hf[c][k], hland.at[h_piece(c), :])

    def weights_send(index, src, dst, device, c):
        return pltpu.make_async_remote_copy(
            src_ref=src,
            dst_ref=dst,
            send_sem=send_sem.at[index],
            recv_sem=recv_sem.at[i_ch[c]],
            device_id=device,
            device_id_type=MESH,
        )

    def weights_cross():
        @pl.when(depth == 0)
        def _():
            for c in range(NC):
                weights_send(i_ex[c], x_piece(c), w_piece(seq, c), cross_dev, c).start()

    def weights_y():
        for k in three:
            send(i_wy[k], w_rows(seq), w_rows(seq), ydev[k])

    oseq = oh * 4 + y

    def weights_pass(c):
        arrived(i_ch[c], w_piece(oseq, c))

        @pl.when(depth == 1)
        def _():
            piece = w_piece(oseq, c)
            for k in three:
                weights_send(i_ps[c][k], piece, piece, pass_dev[k], c).start()

    def weights_relay(c):
        for k in three:
            send(i_wr[c][k], w_piece(oseq, c), w_piece(oseq, c), ydev[k])

    def weights_near():
        for k in three:
            arrived(i_wy[k], w_rows(zh * 4 + yfrom[k]))

    def weights_far(c):
        for k in three:
            arrived(i_wr[c][k], w_piece(oh * 4 + yfrom[k], c))

    def weights_sent():
        @pl.when(depth == 0)
        def _():
            for c in range(NC):
                sent(i_ex[c], x_piece(c))

        @pl.when(depth == 1)
        def _():
            for c in range(NC):
                for k in three:
                    sent(i_ps[c][k], w_piece(oseq, c))

        for k in three:
            sent(i_wy[k], w_rows(seq))
            for c in range(NC):
                sent(i_wr[c][k], w_piece(oseq, c))

    st_slot = lambda v, h: kvs.at[v, half_rows(h), :]

    def stale_tiles():
        local[2].wait()

        def put(tile, values):
            kvs[y, half_rows(zh), tiles[tile]] = values[0]
            sex[:, tiles[tile]] = values[1]

        put(0, both_pairs(straw[0, :, tiles[0]], straw[0, :, tiles[2]]))
        put(1, both_singles(straw[0, :, tiles[1]], straw[1, :, tiles[1]]))
        put(2, both_pairs(straw[1, :, tiles[0]], straw[1, :, tiles[2]]))

    def text_tiles():
        local[3].wait()
        tx[144:256, :] = jnp.zeros((112, 384), BF16)
        live = slice(0, txraw.shape[0])
        tx[live, tiles[0]] = both_pairs(txraw[:, 0, tiles[0]], txraw[:, 0, tiles[2]])[0]
        tx[live, tiles[1]] = both_singles(txraw[:, 0, tiles[1]], txraw[:, 1, tiles[1]])[0]
        tx[live, tiles[2]] = both_pairs(txraw[:, 1, tiles[0]], txraw[:, 1, tiles[2]])[0]

    def stale_z():
        send(i_sz, sex, st_slot(y, zh), zdev)

    def stale_y():
        for k in three:
            send(i_sy[k], st_slot(y, zh), st_slot(y, zh), ydev[k])

    def stale_relay():
        arrived(i_sz, st_slot(y, oh))
        for k in three:
            send(i_sr[k], st_slot(y, oh), st_slot(y, oh), ydev[k])

    def stale_all():
        for k in three:
            arrived(i_sy[k], st_slot(yfrom[k], zh))
            arrived(i_sr[k], st_slot(yfrom[k], oh))

    def stale_sent():
        sent(i_sz, sex)
        for k in three:
            sent(i_sy[k], st_slot(y, zh))
            sent(i_sr[k], st_slot(y, oh))

    def out_send(part):
        for k in three:
            send(i_wo[part][k], wo_h.at[wo_part(0, part), :], wo_rows(tp, part), xdev[k])

    def out_all():
        local[11].wait()
        for k in three:
            for part in range(2):
                arrived(i_wo[part][k], wo_rows(xfrom[k], part))

    def norm_rows(r0, count, shift, scale, store):
        parts = [hx[c, pl.ds(r0, count), :].astype(F32) for c in range(4)]
        total = sum(jnp.sum(part, axis=-1, keepdims=True) for part in parts)
        mean = total * (1.0 / 1536)
        parts = [part - mean for part in parts]
        spread = sum(jnp.sum(part * part, axis=-1, keepdims=True) for part in parts)
        inv = lax.rsqrt(spread * (1.0 / 1536) + 1e-06)
        for c in range(4):
            lanes = slice(c * 384, (c + 1) * 384)
            store(c, (parts[c] * inv * (1.0 + scale(lanes)) + shift(lanes)).astype(BF16))

    def norm_block(h):
        for b in range(4):
            r0 = h * 128 + b * 32

            def store(c, value, r0=r0):
                nm[c // 2, pl.ds(r0, 32), (c % 2) * 384 : (c % 2) * 384 + 384] = value

            norm_rows(r0, 32, lambda l: mod[0, :, l], lambda l: mod[1, :, l], store)

    def go(index):
        pl.semaphore_signal(go_sem.at[index], inc=1, device_id=core, device_id_type=MESH)

    def go_wait(index):
        pl.semaphore_wait(go_sem.at[index], 1)

    @pl.when(sec == 0)
    def _():
        weights_cross()
        hidden_send()
        weights_y()

    @pl.when(sec == 1)
    def _():
        hidden_cross()
        out_send(0)

    stale_tiles()
    for copy in local[4:11]:
        copy.wait()

    @pl.when(sec == 0)
    def _():
        send(i_wf, wf.at[0], wf.at[1], core)
        for c in range(NC):
            weights_pass(c)
            weights_relay(c)
        stale_z()
        out_send(0)
        out_send(1)
        stale_y()
        hidden_own()
        norm_block(zh)
        text_tiles()
        hidden_other()
        norm_block(oh)

    @pl.when(sec == 1)
    def _():
        text_tiles()
        hidden_forward()
        go_wait(0)
        stale_z()
        weights_cross()
        for c in range(NC):
            weights_pass(c)
        go_wait(1)
        weights_y()
        for c in range(NC):
            weights_relay(c)
        stale_y()
        stale_relay()
        go_wait(2)
        out_send(1)
        for n in range(4):
            arrived(i_h1[0][n], hx.at[n, half_rows(zh), :])
        norm_block(zh)
        for n in range(4):
            arrived(i_h1[1][n], hx.at[n, half_rows(oh), :])
        norm_block(oh)

    segment = lax.broadcasted_iota(jnp.int32, (1, 256), 1) // 32
    rank_of = [
        [sum(jnp.where(order[k, s] == p, k, 0) for k in range(1, MICRO)) for p in range(MICRO)]
        for s in range(8)
    ]
    row_segment = lax.broadcasted_iota(jnp.int32, (256, 1), 0) // 32
    qrank = jnp.zeros((256, 1), jnp.int32)
    kranks = []
    for v in range(4):
        krank = jnp.zeros((1, 256), jnp.int32)
        for j in range(8):
            scalar = rank_of[(j // 4) * 4 + v][j % 4]
            krank = jnp.where(segment == j, scalar, krank)
            qrank = jnp.where((row_segment == j) & (y == v), scalar, qrank)
        kranks.append(krank)
    text_live = lax.broadcasted_iota(jnp.int32, (1, 256), 1) < tlen[0]

    weights_near()
    for c in range(5):
        acc[:, tiles[c]] = dot(nm[zh], wv[c, pl.ds(zh * 768, 768), :])
    kv_tile = lambda v, c: kvf.at[v, :, tiles[c]]
    for c in range(5):
        weights_far(c)
        value = acc[:, tiles[c]] + dot(nm[oh], wv[c, pl.ds(oh * 768, 768), :])
        if c < 3:
            kvf[y, :, tiles[c]] = value.astype(BF16)
        else:
            lhs[:, tiles[c - 3]] = value.astype(BF16)
        if c < 3:
            for k in three:
                send(i_kv[c][k], kv_tile(y, c), kv_tile(y, c), ydev[k])
    send(i_nk, kvf.at[y, half_rows(oh), :], nkv, zdev)

    @pl.when(sec == 0)
    def _():
        go(0)
        stale_relay()

    stale_all()
    for c in range(3):
        for k in three:
            arrived(i_kv[c][k], kv_tile(yfrom[k], c))

    @pl.when(sec == 0)
    def _():
        go(1)

    def attend(rb):
        rows = half_rows(rb)
        rank = jnp.where(rb == 0, qrank[0:128], qrank[128:256])
        masks = [kranks[v] <= rank for v in range(4)]
        outs = []
        for j in range(3):
            tile = 0 if j < 2 else 1
            query = lhs[rows, tiles[tile]].astype(F32) * (HEAD ** (-0.5))
            if j == 0:
                keep = low
            elif j == 1:
                keep = jnp.logical_not(low)
            else:
                keep = low == single_low
            query = jnp.where(keep, query, 0.0).astype(BF16)
            kl = tiles[tile]
            vl = tiles[2] if j < 2 else kl
            for v in range(4):
                fresh = dot_nt(query, kvf[v, :, kl])
                stale = dot_nt(query, kvs[v, :, kl])
                sbuf[:, v * 256 : v * 256 + 256] = jnp.where(masks[v], fresh, stale)
            text = dot_nt(query, tx[:, kl])
            sbuf[:, 1024:1280] = jnp.where(text_live, text, -1e30)
            scores = sbuf[...]
            peak = jnp.max(scores, axis=-1, keepdims=True)
            weights = jnp.exp(scores - peak)
            inv = 1.0 / jnp.sum(weights, axis=-1, keepdims=True)
            sbuf[...] = weights * inv
            total = dot(sbuf[:, 1024:1280].astype(BF16), tx[:, vl])
            for v in range(4):
                weights = sbuf[:, v * 256 : v * 256 + 256]
                fresh = jnp.where(masks[v], weights, 0.0).astype(BF16)
                stale = jnp.where(masks[v], 0.0, weights).astype(BF16)
                total = total + dot(fresh, kvf[v, :, vl]) + dot(stale, kvs[v, :, vl])
            outs.append(total)
        at[zh, tp, rb, 0:128, :] = jnp.where(low, outs[0], outs[1]).astype(BF16)
        single = jnp.where(low == single_low, 0.0, outs[2])
        single = single + pltpu.roll(single, HEAD, 1)
        at[zh, tp, rb, 128:192, :] = jnp.where(low, single[0:64], single[64:128]).astype(BF16)

    block = lambda a, x, rb: at.at[a, x, rb]
    attend(oh)
    send(i_az[0], block(zh, tp, oh), block(zh, tp, oh), zdev)

    @pl.when(sec == 0)
    def _():
        for k in three:
            send(i_ax[1][k], block(zh, tp, oh), block(zh, tp, oh), xdev[k])

    attend(zh)

    @pl.when(sec == 0)
    def _():
        send(i_az[1], block(zh, tp, zh), block(zh, tp, zh), zdev)

    for k in three:
        send(i_ax[0][k], block(zh, tp, zh), block(zh, tp, zh), xdev[k])

    arrived(i_nk, nkv)
    mine_kv = [kvf[y, half_rows(zh), tiles[c]] for c in range(3)]
    their_kv = [nkv[:, tiles[c]] for c in range(3)]
    first_kv = [jnp.where(single_low, a, b) for a, b in zip(mine_kv, their_kv)]
    second_kv = [jnp.where(single_low, b, a) for a, b in zip(mine_kv, their_kv)]
    out_kv[0, :, tiles[0]] = first_kv[0]
    out_kv[0, :, tiles[1]] = jnp.where(low, first_kv[1], second_kv[1])
    out_kv[0, :, tiles[2]] = second_kv[0]
    out_kv[1, :, tiles[0]] = first_kv[2]
    out_kv[1, :, tiles[1]] = turn(jnp.where(low, second_kv[1], first_kv[1])).astype(BF16)
    out_kv[1, :, tiles[2]] = second_kv[2]

    arrived(i_az[0], block(oh, tp, zh))
    for k in three:
        send(i_af[0][k], block(oh, tp, zh), block(oh, tp, zh), xdev[k])

    @pl.when(sec == 0)
    def _():
        arrived(i_az[1], block(oh, tp, oh))
        for k in three:
            send(i_af[1][k], block(oh, tp, oh), block(oh, tp, oh), xdev[k])
        for k in three:
            sent(i_hx[k], hid_h)

    def out_rows(part, rb):
        for k in three:
            arrived(i_ax[part][k], block(zh, xfrom[k], rb))
        for k in three:
            arrived(i_af[part][k], block(oh, xfrom[k], rb))
        for x in range(4):
            lhs[0:128, tiles[3 * x]] = at[0, x, rb, 0:128, :]
            lhs[0:128, tiles[3 * x + 2]] = at[1, x, rb, 0:128, :]
            a = at[0, x, rb, 128:192, :]
            b = at[1, x, rb, 128:192, :]
            lhs[0:64, tiles[3 * x + 1]] = jnp.where(low, a.astype(F32), turn(b)).astype(BF16)
            lhs[64:128, tiles[3 * x + 1]] = jnp.where(low, turn(a), b.astype(F32)).astype(BF16)
        for n in range(4):
            lanes = slice(n * 384, n * 384 + 384)
            branch = dot(lhs[0:128, :], wo[:, lanes])
            rows = half_rows(rb)
            hx[n, rows, :] = (hx[n, rows, :].astype(F32) + mod[2, :, lanes] * branch).astype(BF16)

            @pl.when(sec == 0)
            def _():
                send(i_h1[part][n], hx.at[n, rows, :], hx.at[n, rows, :], core)

    out_all()
    out_rows(0, zh)

    @pl.when(sec == 0)
    def _():
        out_rows(1, oh)
        go(2)

    @pl.when(sec == 1)
    def _():
        for b in range(4):

            def store(c, value, b=b):
                fin[b * 32 : b * 32 + 32, c * 384 : c * 384 + 384] = value

            norm_rows(
                zh * 128 + b * 32, 32, lambda l: fmod[0:1, l], lambda l: fmod[1:2, l], store
            )
        arrived(i_wf, wf.at[1])
        theirs = dot_nt(wf[1], fin[...])
        vel[0] = theirs
        send(i_fn, vel.at[0], vel.at[1], core)
        out_lat[...] = lat[...] + step[0] * dot_nt(wf[0], fin[...])

    @pl.when(sec == 0)
    def _():
        arrived(i_fn, vel.at[1])
        out_lat[...] = lat[...] + step[0] * vel[1]

    @pl.when(sec == 0)
    def _():
        for part, rb in ((0, zh), (1, oh)):
            for n in range(4):
                sent(i_h1[part][n], hx.at[n, half_rows(rb), :])
        sent(i_wf, wf.at[0])
        sent(i_az[1], block(zh, tp, zh))
        for k in three:
            sent(i_ax[1][k], block(zh, tp, oh))
            sent(i_af[1][k], block(oh, tp, oh))

    @pl.when(sec == 1)
    def _():
        sent(i_fn, vel.at[0])
        hidden_sent()

    weights_sent()
    stale_sent()
    for k in three:
        for part in range(2):
            sent(i_wo[part][k], wo_rows(tp, part))
        for c in range(3):
            sent(i_kv[c][k], kv_tile(y, c))
        sent(i_ax[0][k], block(zh, tp, zh))
        sent(i_af[0][k], block(oh, tp, zh))
    sent(i_nk, nkv)
    sent(i_az[0], block(zh, tp, oh))


def body(
    hidden, latent, w_qkv, w_out, modulation, final_mod, w_final, stale_kv, text_kv, text_len,
    patch_order, step_size,
):
    vmem = pl.BlockSpec(memory_space=pltpu.VMEM)
    any_ = pl.BlockSpec(memory_space=pltpu.HBM)
    text = text_kv[0].transpose(1, 0, 2)
    lat_next, kv_next = pl.pallas_call(
        kernel,
        out_shape=(
            jax.ShapeDtypeStruct((8, 128), F32),
            jax.ShapeDtypeStruct((2, 128, 384), BF16),
        ),
        in_specs=[any_] * 12,
        out_specs=(vmem, vmem),
        scratch_shapes=[
            pltpu.VMEM((4, 256, 384), BF16),
            pltpu.VMEM((128, 384), BF16),
            pltpu.VMEM((3, 192, 384), BF16),
            pltpu.VMEM((5, 192, 128), BF16),
            pltpu.VMEM((5, 1536, 128), BF16),
            pltpu.VMEM((4, 256, 384), BF16),
            pltpu.VMEM((4, 256, 384), BF16),
            pltpu.VMEM((2, 128, 384), BF16),
            pltpu.VMEM((128, 384), BF16),
            pltpu.VMEM(text.shape, BF16),
            pltpu.VMEM((256, 384), BF16),
            pltpu.VMEM((1536, 1536), BF16),
            pltpu.VMEM((2, 256, 768), BF16),
            pltpu.VMEM((2, 4, 2, 192, 128), BF16),
            pltpu.VMEM((256, 1536), BF16),
            pltpu.VMEM((128, 384), BF16),
            pltpu.VMEM((128, 1536), BF16),
            pltpu.VMEM((256, 640), F32),
            pltpu.VMEM((128, 1280), F32),
            pltpu.VMEM((3, 1, 1536), F32),
            pltpu.VMEM((2, 1536), F32),
            pltpu.VMEM((2, 8, 1536), BF16),
            pltpu.VMEM((2, 8, 128), F32),
            pltpu.VMEM((8, 128), F32),
            pltpu.SMEM((4, 8), jnp.int32),
            pltpu.SMEM((1,), jnp.int32),
            pltpu.SMEM((1,), F32),
            pltpu.SemaphoreType.DMA((N_LINK,)),
            pltpu.SemaphoreType.DMA((N_LINK,)),
            pltpu.SemaphoreType.DMA((N_LOCAL,)),
            pltpu.SemaphoreType.REGULAR((3,)),
        ],
        compiler_params=pltpu.CompilerParams(
            collective_id=0, has_side_effects=True, vmem_limit_bytes=63 << 20
        ),
        name="both_layers",
    )(
        patch_order.T, text_len, step_size, hidden, w_qkv[0].transpose(1, 0, 2), w_out[0],
        stale_kv[0], text, modulation.transpose(1, 0, 2), final_mod, w_final.T, latent.T,
    )
    return lat_next.T, kv_next[None]


def solution(mesh):
    return jax.shard_map(
        body,
        mesh=mesh,
        in_specs=(
            P(("req", "seq"), "tp"),
            P(("req", "seq"), ("section", "tp")),
            P("section", "seq", None, "tp"),
            P("section", "tp", None),
            P("section", None, None),
            P(),
            P(None, ("section", "tp")),
            P("section", None, ("req", "seq"), "tp"),
            P("section", None, "req", "tp"),
            P("req"),
            P("req", None),
            P(),
        ),
        out_specs=(P(("req", "seq"), ("section", "tp")), P("section", None, ("req", "seq"), "tp")),
        check_vma=False,
    )
```

```python
import jax
import jax.numpy as jnp
from jax import lax
from jax.experimental import pallas as pl
from jax.experimental.pallas import tpu as pltpu
from jax.sharding import PartitionSpec as P

HEAD = 64
MICRO = 4
NC = 5
HC = 2
MESH = pl.DeviceIdType.MESH
F32 = jnp.float32
BF16 = jnp.bfloat16


def dot(a, b):
    return jnp.dot(a, b, preferred_element_type=F32)


def dot_nt(a, b):
    return lax.dot_general(a, b, (((1,), (1,)), ((), ())), preferred_element_type=F32)


class Link:
    def __init__(self, send_sem, recv_sem):
        self.send_sem, self.recv_sem, self.used = send_sem, recv_sem, 0

    def take(self):
        index = self.used
        self.used += 1
        return index

    def make(self, index, src, dst, device):
        return pltpu.make_async_remote_copy(
            src_ref=src,
            dst_ref=dst,
            send_sem=self.send_sem.at[index],
            recv_sem=self.recv_sem.at[index],
            device_id=device,
            device_id_type=MESH,
        )


N_LINK = 112
N_LOCAL = 12


def kernel(
    order_h, tlen_h, step_h, hid_h, wq_h, wo_h, st_h, tx_h, mod_h, fmod_h, wf_h, lat_h,
    out_lat, out_kv,
    hx, hland, wraw, wex, wv, kvf, kvs, straw, sex, txraw, tx, wo, nm, at, lhs, nkv, fin, acc, sbuf,
    mod, fmod, wf, vel, lat, order, tlen, step,
    send_sem, recv_sem, loc_sem, go_sem,
):
    sec = lax.axis_index("section")
    seq = lax.axis_index("seq")
    tp = lax.axis_index("tp")
    req = lax.axis_index("req")
    zh = seq // 4
    oh = 1 - zh
    y = seq % 4
    z = zh * 8 + req
    far = req // 4
    hop = 1 - 2 * far
    depth = req + far * (7 - 2 * req)
    xs = [(tp + k) % 4 for k in (1, 2, 3)]
    ys = [(y + k) % 4 for k in (1, 2, 3)]
    xfrom = [(tp + 4 - k) % 4 for k in (1, 2, 3)]
    yfrom = [(y + 4 - k) % 4 for k in (1, 2, 3)]
    xdev = [{"tp": v} for v in xs]
    ydev = [{"seq": zh * 4 + v} for v in ys]
    zdev = {"seq": (seq + 4) % 8}
    core = {"section": 1 - sec}
    xcross = [{"tp": v, "section": 1 - sec} for v in xs]

    def along_z(steps):
        place = (z + steps + 16) % 16
        return {"seq": (place // 8) * 4 + y, "req": place % 8}

    cross_dev = along_z(-2 * hop)
    pass_dev = [along_z(hop), along_z(2 * hop), along_z(-hop)]

    barrier = pltpu.get_barrier_semaphore()
    for device in xdev + xcross + ydev + [zdev, core, cross_dev] + pass_dev:
        pl.semaphore_signal(barrier, inc=1, device_id=device, device_id_type=MESH)

    link = Link(send_sem, recv_sem)
    half_rows = lambda h: pl.ds(h * 128, 128)
    three = range(3)
    i_hx = [link.take() for _ in three]
    i_hz = [link.take() for _ in range(HC)]
    i_hf = [[link.take() for _ in range(4)] for _ in range(HC)]
    i_wy = [link.take() for _ in three]
    i_ch = [link.take() for _ in range(NC)]
    i_ex = [link.take() for _ in range(NC)]
    i_ps = [[link.take() for _ in three] for _ in range(NC)]
    i_wr = [[link.take() for _ in three] for _ in range(NC)]
    i_sy = [link.take() for _ in three]
    i_sz = link.take()
    i_sr = [link.take() for _ in three]
    i_wo = [[link.take() for _ in three] for _ in range(2)]
    i_kv = [[link.take() for _ in three] for _ in range(3)]
    i_nk = link.take()
    i_ax = [[link.take() for _ in three] for _ in range(2)]
    i_az = [link.take() for _ in range(2)]
    i_af = [[link.take() for _ in three] for _ in range(2)]
    i_h1 = [[link.take() for _ in range(4)] for _ in range(2)]
    i_fn = link.take()
    i_wf = link.take()

    def send(index, src, dst, device):
        link.make(index, src, dst, device).start()

    def arrived(index, dst):
        link.make(index, dst, dst, core).wait_recv()

    def sent(index, src):
        link.make(index, src, src, core).wait_send()

    hx_slot = lambda x, h: hx.at[x, half_rows(h), :]

    wo_part = lambda start, part: pl.ds(start + part * 96, (96, 288)[part])
    wo_rows = lambda x, part: wo.at[wo_part(x * 384, part), :]
    local = [
        pltpu.make_async_copy(src, dst, loc_sem.at[n])
        for n, (src, dst) in enumerate(
            [
                (wq_h, wraw),
                (hid_h, hx_slot(tp, zh)),
                (st_h, straw),
                (tx_h, txraw),
                (mod_h, mod),
                (order_h, order),
                (tlen_h, tlen),
                (step_h, step),
                (fmod_h, fmod),
                (wf_h, wf.at[0]),
                (lat_h, lat),
                (wo_h, wo.at[pl.ds(tp * 384, 384), :]),
            ]
        )
    ]
    local[0].start()

    @pl.when(sec == 0)
    def _():
        local[1].start()

    for copy in local[2:]:
        copy.start()

    low = lax.broadcasted_iota(jnp.int32, (1, 128), 1) < HEAD
    single_low = zh == 0
    tiles = [slice(c * 128, c * 128 + 128) for c in range(12)]

    def turn(value):
        return pltpu.roll(value.astype(F32), HEAD, 1)

    def both_singles(k_tile, v_tile):
        turned = turn(v_tile)
        k_tile = k_tile.astype(F32)
        zero = jnp.where(low, k_tile, turned).astype(BF16)
        one = jnp.where(low, turned, k_tile).astype(BF16)
        return jnp.where(single_low, zero, one), jnp.where(single_low, one, zero)

    def both_pairs(first, last):
        return jnp.where(single_low, first, last), jnp.where(single_low, last, first)

    w_rows = lambda s: wv.at[:, pl.ds(s * 192, 192), :]
    w_piece = lambda s, c: wv.at[c, pl.ds(s * 192, 192), :]
    x_piece = lambda c: wex.at[c]

    def put_w(tile, values):
        wv[tile, pl.ds(seq * 192, 192), :] = values[0]
        wex[tile] = values[1]

    local[0].wait()
    put_w(0, both_pairs(wraw[1, :, tiles[0]], wraw[1, :, tiles[2]]))
    put_w(1, both_singles(wraw[1, :, tiles[1]], wraw[2, :, tiles[1]]))
    put_w(2, both_pairs(wraw[2, :, tiles[0]], wraw[2, :, tiles[2]]))
    put_w(3, both_pairs(wraw[0, :, tiles[0]], wraw[0, :, tiles[2]]))
    put_w(4, [wraw[0, :, tiles[1]]] * 2)

    pl.semaphore_wait(barrier, 15)

    HR = 128 // HC
    h_piece = lambda c: pl.ds(c * HR, HR)
    h_slot = lambda x, h, c: hx.at[x, pl.ds(h * 128 + c * HR, HR), :]

    def hidden_send():
        for k in three:
            send(i_hx[k], hid_h, hx_slot(tp, zh), xdev[k])

    def hidden_own():
        local[1].wait()
        for k in three:
            arrived(i_hx[k], hx_slot(xfrom[k], zh))

    def hidden_cross():
        for c in range(HC):
            send(i_hz[c], hid_h.at[h_piece(c), :], hland.at[h_piece(c), :], zdev)

    def hidden_forward():
        for c in range(HC):
            arrived(i_hz[c], hland.at[h_piece(c), :])
            for k, device in enumerate(xcross + [core]):
                send(i_hf[c][k], hland.at[h_piece(c), :], h_slot(tp, oh, c), device)

    def hidden_other():
        for c in range(HC):
            for k in range(4):
                arrived(i_hf[c][k], h_slot((xfrom + [tp])[k], oh, c))

    def hidden_sent():
        for c in range(HC):
            sent(i_hz[c], hid_h.at[h_piece(c), :])
            for k in range(4):
                sent(i_hf[c][k], hland.at[h_piece(c), :])

    def weights_send(index, src, dst, device, c):
        return pltpu.make_async_remote_copy(
            src_ref=src,
            dst_ref=dst,
            send_sem=send_sem.at[index],
            recv_sem=recv_sem.at[i_ch[c]],
            device_id=device,
            device_id_type=MESH,
        )

    def weights_cross():
        @pl.when(depth == 0)
        def _():
            for c in range(NC):
                weights_send(i_ex[c], x_piece(c), w_piece(seq, c), cross_dev, c).start()

    def weights_y():
        for k in three:
            send(i_wy[k], w_rows(seq), w_rows(seq), ydev[k])

    oseq = oh * 4 + y

    def weights_pass(c):
        arrived(i_ch[c], w_piece(oseq, c))

        @pl.when(depth == 1)
        def _():
            piece = w_piece(oseq, c)
            for k in three:
                weights_send(i_ps[c][k], piece, piece, pass_dev[k], c).start()

    def weights_relay(c):
        for k in three:
            send(i_wr[c][k], w_piece(oseq, c), w_piece(oseq, c), ydev[k])

    def weights_near():
        for k in three:
            arrived(i_wy[k], w_rows(zh * 4 + yfrom[k]))

    def weights_far(c):
        for k in three:
            arrived(i_wr[c][k], w_piece(oh * 4 + yfrom[k], c))

    def weights_sent():
        @pl.when(depth == 0)
        def _():
            for c in range(NC):
                sent(i_ex[c], x_piece(c))

        @pl.when(depth == 1)
        def _():
            for c in range(NC):
                for k in three:
                    sent(i_ps[c][k], w_piece(oseq, c))

        for k in three:
            sent(i_wy[k], w_rows(seq))
            for c in range(NC):
                sent(i_wr[c][k], w_piece(oseq, c))

    st_slot = lambda v, h: kvs.at[v, half_rows(h), :]

    def stale_tiles():
        local[2].wait()

        def put(tile, values):
            kvs[y, half_rows(zh), tiles[tile]] = values[0]
            sex[:, tiles[tile]] = values[1]

        put(0, both_pairs(straw[0, :, tiles[0]], straw[0, :, tiles[2]]))
        put(1, both_singles(straw[0, :, tiles[1]], straw[1, :, tiles[1]]))
        put(2, both_pairs(straw[1, :, tiles[0]], straw[1, :, tiles[2]]))

    def text_tiles():
        local[3].wait()
        tx[144:256, :] = jnp.zeros((112, 384), BF16)
        live = slice(0, txraw.shape[0])
        tx[live, tiles[0]] = both_pairs(txraw[:, 0, tiles[0]], txraw[:, 0, tiles[2]])[0]
        tx[live, tiles[1]] = both_singles(txraw[:, 0, tiles[1]], txraw[:, 1, tiles[1]])[0]
        tx[live, tiles[2]] = both_pairs(txraw[:, 1, tiles[0]], txraw[:, 1, tiles[2]])[0]

    def stale_z():
        send(i_sz, sex, st_slot(y, zh), zdev)

    def stale_y():
        for k in three:
            send(i_sy[k], st_slot(y, zh), st_slot(y, zh), ydev[k])

    def stale_relay():
        arrived(i_sz, st_slot(y, oh))
        for k in three:
            send(i_sr[k], st_slot(y, oh), st_slot(y, oh), ydev[k])

    def stale_all():
        for k in three:
            arrived(i_sy[k], st_slot(yfrom[k], zh))
            arrived(i_sr[k], st_slot(yfrom[k], oh))

    def stale_sent():
        sent(i_sz, sex)
        for k in three:
            sent(i_sy[k], st_slot(y, zh))
            sent(i_sr[k], st_slot(y, oh))

    def out_send(part):
        for k in three:
            send(i_wo[part][k], wo_h.at[wo_part(0, part), :], wo_rows(tp, part), xdev[k])

    def out_all():
        local[11].wait()
        for k in three:
            for part in range(2):
                arrived(i_wo[part][k], wo_rows(xfrom[k], part))

    def norm_rows(r0, count, shift, scale, store):
        parts = [hx[c, pl.ds(r0, count), :].astype(F32) for c in range(4)]
        total = sum(jnp.sum(part, axis=-1, keepdims=True) for part in parts)
        mean = total * (1.0 / 1536)
        parts = [part - mean for part in parts]
        spread = sum(jnp.sum(part * part, axis=-1, keepdims=True) for part in parts)
        inv = lax.rsqrt(spread * (1.0 / 1536) + 1e-06)
        for c in range(4):
            lanes = slice(c * 384, (c + 1) * 384)
            store(c, (parts[c] * inv * (1.0 + scale(lanes)) + shift(lanes)).astype(BF16))

    def norm_block(h):
        for b in range(4):
            r0 = h * 128 + b * 32

            def store(c, value, r0=r0):
                nm[c // 2, pl.ds(r0, 32), (c % 2) * 384 : (c % 2) * 384 + 384] = value

            norm_rows(r0, 32, lambda l: mod[0, :, l], lambda l: mod[1, :, l], store)

    def go(index):
        pl.semaphore_signal(go_sem.at[index], inc=1, device_id=core, device_id_type=MESH)

    def go_wait(index):
        pl.semaphore_wait(go_sem.at[index], 1)

    @pl.when(sec == 0)
    def _():
        weights_cross()
        hidden_send()
        weights_y()

    @pl.when(sec == 1)
    def _():
        hidden_cross()
        out_send(0)

    stale_tiles()
    for copy in local[4:11]:
        copy.wait()

    @pl.when(sec == 0)
    def _():
        send(i_wf, wf.at[0], wf.at[1], core)
        for c in range(NC):
            weights_pass(c)
            weights_relay(c)
        stale_z()
        out_send(0)
        out_send(1)
        stale_y()
        hidden_own()
        norm_block(zh)
        text_tiles()
        hidden_other()
        norm_block(oh)

    @pl.when(sec == 1)
    def _():
        text_tiles()
        hidden_forward()
        go_wait(0)
        stale_z()
        weights_cross()

        @pl.when(depth == 1)
        def _():
            for c in range(NC):
                weights_pass(c)

        go_wait(1)
        weights_y()
        stale_y()

        @pl.when(depth != 1)
        def _():
            for c in range(NC):
                arrived(i_ch[c], w_piece(oseq, c))

        for c in range(NC):
            weights_relay(c)
        stale_relay()
        go_wait(2)
        out_send(1)
        for n in range(4):
            arrived(i_h1[0][n], hx.at[n, half_rows(zh), :])
        norm_block(zh)
        for n in range(4):
            arrived(i_h1[1][n], hx.at[n, half_rows(oh), :])
        norm_block(oh)

    segment = lax.broadcasted_iota(jnp.int32, (1, 256), 1) // 32
    rank_of = [
        [sum(jnp.where(order[k, s] == p, k, 0) for k in range(1, MICRO)) for p in range(MICRO)]
        for s in range(8)
    ]
    row_segment = lax.broadcasted_iota(jnp.int32, (256, 1), 0) // 32
    qrank = jnp.zeros((256, 1), jnp.int32)
    kranks = []
    for v in range(4):
        krank = jnp.zeros((1, 256), jnp.int32)
        for j in range(8):
            scalar = rank_of[(j // 4) * 4 + v][j % 4]
            krank = jnp.where(segment == j, scalar, krank)
            qrank = jnp.where((row_segment == j) & (y == v), scalar, qrank)
        kranks.append(krank)
    text_live = lax.broadcasted_iota(jnp.int32, (1, 256), 1) < tlen[0]

    weights_near()
    for c in range(5):
        acc[:, tiles[c]] = dot(nm[zh], wv[c, pl.ds(zh * 768, 768), :])
    kv_tile = lambda v, c: kvf.at[v, :, tiles[c]]
    for c in range(5):
        weights_far(c)
        value = acc[:, tiles[c]] + dot(nm[oh], wv[c, pl.ds(oh * 768, 768), :])
        if c < 3:
            kvf[y, :, tiles[c]] = value.astype(BF16)
        else:
            lhs[:, tiles[c - 3]] = value.astype(BF16)
        if c < 3:
            for k in three:
                send(i_kv[c][k], kv_tile(y, c), kv_tile(y, c), ydev[k])
    send(i_nk, kvf.at[y, half_rows(oh), :], nkv, zdev)

    @pl.when(sec == 0)
    def _():
        go(0)
        stale_relay()

    stale_all()
    for c in range(3):
        for k in three:
            arrived(i_kv[c][k], kv_tile(yfrom[k], c))

    @pl.when(sec == 0)
    def _():
        go(1)

    def attend(rb):
        rows = half_rows(rb)
        rank = jnp.where(rb == 0, qrank[0:128], qrank[128:256])
        masks = [kranks[v] <= rank for v in range(4)]
        outs = []
        for j in range(3):
            tile = 0 if j < 2 else 1
            query = lhs[rows, tiles[tile]].astype(F32) * (HEAD ** (-0.5))
            if j == 0:
                keep = low
            elif j == 1:
                keep = jnp.logical_not(low)
            else:
                keep = low == single_low
            query = jnp.where(keep, query, 0.0).astype(BF16)
            kl = tiles[tile]
            vl = tiles[2] if j < 2 else kl
            for v in range(4):
                fresh = dot_nt(query, kvf[v, :, kl])
                stale = dot_nt(query, kvs[v, :, kl])
                sbuf[:, v * 256 : v * 256 + 256] = jnp.where(masks[v], fresh, stale)
            text = dot_nt(query, tx[:, kl])
            sbuf[:, 1024:1280] = jnp.where(text_live, text, -1e30)
            scores = sbuf[...]
            peak = jnp.max(scores, axis=-1, keepdims=True)
            weights = jnp.exp(scores - peak)
            inv = 1.0 / jnp.sum(weights, axis=-1, keepdims=True)
            sbuf[...] = weights * inv
            total = dot(sbuf[:, 1024:1280].astype(BF16), tx[:, vl])
            for v in range(4):
                weights = sbuf[:, v * 256 : v * 256 + 256]
                fresh = jnp.where(masks[v], weights, 0.0).astype(BF16)
                stale = jnp.where(masks[v], 0.0, weights).astype(BF16)
                total = total + dot(fresh, kvf[v, :, vl]) + dot(stale, kvs[v, :, vl])
            outs.append(total)
        at[zh, tp, rb, 0:128, :] = jnp.where(low, outs[0], outs[1]).astype(BF16)
        single = jnp.where(low == single_low, 0.0, outs[2])
        single = single + pltpu.roll(single, HEAD, 1)
        at[zh, tp, rb, 128:192, :] = jnp.where(low, single[0:64], single[64:128]).astype(BF16)

    block = lambda a, x, rb: at.at[a, x, rb]
    attend(oh)
    send(i_az[0], block(zh, tp, oh), block(zh, tp, oh), zdev)

    @pl.when(sec == 0)
    def _():
        for k in three:
            send(i_ax[1][k], block(zh, tp, oh), block(zh, tp, oh), xdev[k])

    attend(zh)

    @pl.when(sec == 0)
    def _():
        send(i_az[1], block(zh, tp, zh), block(zh, tp, zh), zdev)

    for k in three:
        send(i_ax[0][k], block(zh, tp, zh), block(zh, tp, zh), xdev[k])

    arrived(i_nk, nkv)
    mine_kv = [kvf[y, half_rows(zh), tiles[c]] for c in range(3)]
    their_kv = [nkv[:, tiles[c]] for c in range(3)]
    first_kv = [jnp.where(single_low, a, b) for a, b in zip(mine_kv, their_kv)]
    second_kv = [jnp.where(single_low, b, a) for a, b in zip(mine_kv, their_kv)]
    out_kv[0, :, tiles[0]] = first_kv[0]
    out_kv[0, :, tiles[1]] = jnp.where(low, first_kv[1], second_kv[1])
    out_kv[0, :, tiles[2]] = second_kv[0]
    out_kv[1, :, tiles[0]] = first_kv[2]
    out_kv[1, :, tiles[1]] = turn(jnp.where(low, second_kv[1], first_kv[1])).astype(BF16)
    out_kv[1, :, tiles[2]] = second_kv[2]

    arrived(i_az[0], block(oh, tp, zh))
    for k in three:
        send(i_af[0][k], block(oh, tp, zh), block(oh, tp, zh), xdev[k])

    @pl.when(sec == 0)
    def _():
        arrived(i_az[1], block(oh, tp, oh))
        for k in three:
            send(i_af[1][k], block(oh, tp, oh), block(oh, tp, oh), xdev[k])
        for k in three:
            sent(i_hx[k], hid_h)

    def out_rows(part, rb):
        for k in three:
            arrived(i_ax[part][k], block(zh, xfrom[k], rb))
        for k in three:
            arrived(i_af[part][k], block(oh, xfrom[k], rb))
        for x in range(4):
            lhs[0:128, tiles[3 * x]] = at[0, x, rb, 0:128, :]
            lhs[0:128, tiles[3 * x + 2]] = at[1, x, rb, 0:128, :]
            a = at[0, x, rb, 128:192, :]
            b = at[1, x, rb, 128:192, :]
            lhs[0:64, tiles[3 * x + 1]] = jnp.where(low, a.astype(F32), turn(b)).astype(BF16)
            lhs[64:128, tiles[3 * x + 1]] = jnp.where(low, turn(a), b.astype(F32)).astype(BF16)
        for n in range(4):
            lanes = slice(n * 384, n * 384 + 384)
            branch = dot(lhs[0:128, :], wo[:, lanes])
            rows = half_rows(rb)
            hx[n, rows, :] = (hx[n, rows, :].astype(F32) + mod[2, :, lanes] * branch).astype(BF16)

            @pl.when(sec == 0)
            def _():
                send(i_h1[part][n], hx.at[n, rows, :], hx.at[n, rows, :], core)

    out_all()
    out_rows(0, zh)

    @pl.when(sec == 0)
    def _():
        out_rows(1, oh)
        go(2)

    @pl.when(sec == 1)
    def _():
        for b in range(4):

            def store(c, value, b=b):
                fin[b * 32 : b * 32 + 32, c * 384 : c * 384 + 384] = value

            norm_rows(
                zh * 128 + b * 32, 32, lambda l: fmod[0:1, l], lambda l: fmod[1:2, l], store
            )
        arrived(i_wf, wf.at[1])
        theirs = dot_nt(wf[1], fin[...])
        vel[0] = theirs
        send(i_fn, vel.at[0], vel.at[1], core)
        out_lat[...] = lat[...] + step[0] * dot_nt(wf[0], fin[...])

    @pl.when(sec == 0)
    def _():
        arrived(i_fn, vel.at[1])
        out_lat[...] = lat[...] + step[0] * vel[1]

    @pl.when(sec == 0)
    def _():
        for part, rb in ((0, zh), (1, oh)):
            for n in range(4):
                sent(i_h1[part][n], hx.at[n, half_rows(rb), :])
        sent(i_wf, wf.at[0])
        sent(i_az[1], block(zh, tp, zh))
        for k in three:
            sent(i_ax[1][k], block(zh, tp, oh))
            sent(i_af[1][k], block(oh, tp, oh))

    @pl.when(sec == 1)
    def _():
        sent(i_fn, vel.at[0])
        hidden_sent()

    weights_sent()
    stale_sent()
    for k in three:
        for part in range(2):
            sent(i_wo[part][k], wo_rows(tp, part))
        for c in range(3):
            sent(i_kv[c][k], kv_tile(y, c))
        sent(i_ax[0][k], block(zh, tp, zh))
        sent(i_af[0][k], block(oh, tp, zh))
    sent(i_nk, nkv)
    sent(i_az[0], block(zh, tp, oh))


def body(
    hidden, latent, w_qkv, w_out, modulation, final_mod, w_final, stale_kv, text_kv, text_len,
    patch_order, step_size,
):
    vmem = pl.BlockSpec(memory_space=pltpu.VMEM)
    any_ = pl.BlockSpec(memory_space=pltpu.HBM)
    text = text_kv[0].transpose(1, 0, 2)
    lat_next, kv_next = pl.pallas_call(
        kernel,
        out_shape=(
            jax.ShapeDtypeStruct((8, 128), F32),
            jax.ShapeDtypeStruct((2, 128, 384), BF16),
        ),
        in_specs=[any_] * 12,
        out_specs=(vmem, vmem),
        scratch_shapes=[
            pltpu.VMEM((4, 256, 384), BF16),
            pltpu.VMEM((128, 384), BF16),
            pltpu.VMEM((3, 192, 384), BF16),
            pltpu.VMEM((5, 192, 128), BF16),
            pltpu.VMEM((5, 1536, 128), BF16),
            pltpu.VMEM((4, 256, 384), BF16),
            pltpu.VMEM((4, 256, 384), BF16),
            pltpu.VMEM((2, 128, 384), BF16),
            pltpu.VMEM((128, 384), BF16),
            pltpu.VMEM(text.shape, BF16),
            pltpu.VMEM((256, 384), BF16),
            pltpu.VMEM((1536, 1536), BF16),
            pltpu.VMEM((2, 256, 768), BF16),
            pltpu.VMEM((2, 4, 2, 192, 128), BF16),
            pltpu.VMEM((256, 1536), BF16),
            pltpu.VMEM((128, 384), BF16),
            pltpu.VMEM((128, 1536), BF16),
            pltpu.VMEM((256, 640), F32),
            pltpu.VMEM((128, 1280), F32),
            pltpu.VMEM((3, 1, 1536), F32),
            pltpu.VMEM((2, 1536), F32),
            pltpu.VMEM((2, 8, 1536), BF16),
            pltpu.VMEM((2, 8, 128), F32),
            pltpu.VMEM((8, 128), F32),
            pltpu.SMEM((4, 8), jnp.int32),
            pltpu.SMEM((1,), jnp.int32),
            pltpu.SMEM((1,), F32),
            pltpu.SemaphoreType.DMA((N_LINK,)),
            pltpu.SemaphoreType.DMA((N_LINK,)),
            pltpu.SemaphoreType.DMA((N_LOCAL,)),
            pltpu.SemaphoreType.REGULAR((3,)),
        ],
        compiler_params=pltpu.CompilerParams(
            collective_id=0, has_side_effects=True, vmem_limit_bytes=48 << 20
        ),
        name="both_layers",
    )(
        *[
            pltpu.with_memory_space_constraint(value, pltpu.HBM) if value.ndim > 1 else value
            for value in (
                patch_order.T, text_len, step_size, hidden, w_qkv[0].transpose(1, 0, 2), w_out[0],
                stale_kv[0], text, modulation.transpose(1, 0, 2), final_mod, w_final.T, latent.T,
            )
        ]
    )
    return lat_next.T, kv_next[None]


def solution(mesh):
    return jax.shard_map(
        body,
        mesh=mesh,
        in_specs=(
            P(("req", "seq"), "tp"),
            P(("req", "seq"), ("section", "tp")),
            P("section", "seq", None, "tp"),
            P("section", "tp", None),
            P("section", None, None),
            P(),
            P(None, ("section", "tp")),
            P("section", None, ("req", "seq"), "tp"),
            P("section", None, "req", "tp"),
            P("req"),
            P("req", None),
            P(),
        ),
        out_specs=(P(("req", "seq"), ("section", "tp")), P("section", None, ("req", "seq"), "tp")),
        check_vma=False,
    )
```

```python
import jax
import jax.numpy as jnp
from jax import lax
from jax.experimental import pallas as pl
from jax.experimental.pallas import tpu as pltpu
from jax.sharding import PartitionSpec as P

HEAD = 64
MICRO = 4
NC = 5
HC = 2
MESH = pl.DeviceIdType.MESH
F32 = jnp.float32
BF16 = jnp.bfloat16


def dot(a, b):
    return jnp.dot(a, b, preferred_element_type=F32)


def dot_nt(a, b):
    return lax.dot_general(a, b, (((1,), (1,)), ((), ())), preferred_element_type=F32)


class Link:
    def __init__(self, send_sem, recv_sem):
        self.send_sem, self.recv_sem, self.used = send_sem, recv_sem, 0

    def take(self):
        index = self.used
        self.used += 1
        return index

    def make(self, index, src, dst, device):
        return pltpu.make_async_remote_copy(
            src_ref=src,
            dst_ref=dst,
            send_sem=self.send_sem.at[index],
            recv_sem=self.recv_sem.at[index],
            device_id=device,
            device_id_type=MESH,
        )


N_LINK = 112
N_LOCAL = 12


def kernel(
    order_h, tlen_h, step_h, hid_h, wq_h, wo_h, st_h, tx_h, mod_h, fmod_h, wf_h, lat_h,
    out_lat, out_kv,
    hx, hland, wraw, wex, wv, kvf, kvs, straw, sex, txraw, tx, wo, nm, at, lhs, nkv, fin, acc, sbuf,
    mod, fmod, wf, vel, lat, order, tlen, step,
    send_sem, recv_sem, loc_sem, go_sem,
):
    sec = lax.axis_index("section")
    seq = lax.axis_index("seq")
    tp = lax.axis_index("tp")
    req = lax.axis_index("req")
    zh = seq // 4
    oh = 1 - zh
    y = seq % 4
    z = zh * 8 + req
    far = req // 4
    hop = 1 - 2 * far
    depth = req + far * (7 - 2 * req)
    xs = [(tp + k) % 4 for k in (1, 2, 3)]
    ys = [(y + k) % 4 for k in (1, 2, 3)]
    xfrom = [(tp + 4 - k) % 4 for k in (1, 2, 3)]
    yfrom = [(y + 4 - k) % 4 for k in (1, 2, 3)]
    xdev = [{"tp": v} for v in xs]
    ydev = [{"seq": zh * 4 + v} for v in ys]
    zdev = {"seq": (seq + 4) % 8}
    core = {"section": 1 - sec}
    xcross = [{"tp": v, "section": 1 - sec} for v in xs]

    def along_z(steps):
        place = (z + steps + 16) % 16
        return {"seq": (place // 8) * 4 + y, "req": place % 8}

    cross_dev = along_z(-2 * hop)
    pass_dev = [along_z(-hop), along_z(2 * hop), along_z(hop)]

    barrier = pltpu.get_barrier_semaphore()
    for device in xdev + xcross + ydev + [zdev, core, cross_dev] + pass_dev:
        pl.semaphore_signal(barrier, inc=1, device_id=device, device_id_type=MESH)

    link = Link(send_sem, recv_sem)
    half_rows = lambda h: pl.ds(h * 128, 128)
    three = range(3)
    i_hx = [link.take() for _ in three]
    i_hz = [link.take() for _ in range(HC)]
    i_hf = [[link.take() for _ in range(4)] for _ in range(HC)]
    i_wy = [link.take() for _ in three]
    i_ch = [link.take() for _ in range(NC)]
    i_ex = [link.take() for _ in range(NC)]
    i_ps = [[link.take() for _ in three] for _ in range(NC)]
    i_wr = [[link.take() for _ in three] for _ in range(NC)]
    i_sy = [link.take() for _ in three]
    i_sz = link.take()
    i_sr = [link.take() for _ in three]
    i_wo = [[link.take() for _ in three] for _ in range(2)]
    i_kv = [[link.take() for _ in three] for _ in range(3)]
    i_nk = link.take()
    i_ax = [[link.take() for _ in three] for _ in range(2)]
    i_az = [link.take() for _ in range(2)]
    i_af = [[link.take() for _ in three] for _ in range(2)]
    i_h1 = [[link.take() for _ in range(4)] for _ in range(2)]
    i_fn = link.take()
    i_wf = link.take()

    def send(index, src, dst, device):
        link.make(index, src, dst, device).start()

    def arrived(index, dst):
        link.make(index, dst, dst, core).wait_recv()

    def sent(index, src):
        link.make(index, src, src, core).wait_send()

    hx_slot = lambda x, h: hx.at[x, half_rows(h), :]

    wo_part = lambda start, part: pl.ds(start + part * 96, (96, 288)[part])
    wo_rows = lambda x, part: wo.at[wo_part(x * 384, part), :]
    local = [
        pltpu.make_async_copy(src, dst, loc_sem.at[n])
        for n, (src, dst) in enumerate(
            [
                (wq_h, wraw),
                (hid_h, hx_slot(tp, zh)),
                (st_h, straw),
                (tx_h, txraw),
                (mod_h, mod),
                (order_h, order),
                (tlen_h, tlen),
                (step_h, step),
                (fmod_h, fmod),
                (wf_h, wf.at[0]),
                (lat_h, lat),
                (wo_h, wo.at[pl.ds(tp * 384, 384), :]),
            ]
        )
    ]
    local[0].start()

    @pl.when(sec == 0)
    def _():
        local[1].start()

    for copy in local[2:]:
        copy.start()

    low = lax.broadcasted_iota(jnp.int32, (1, 128), 1) < HEAD
    single_low = zh == 0
    tiles = [slice(c * 128, c * 128 + 128) for c in range(12)]

    def turn(value):
        return pltpu.roll(value.astype(F32), HEAD, 1)

    def both_singles(k_tile, v_tile):
        turned = turn(v_tile)
        k_tile = k_tile.astype(F32)
        zero = jnp.where(low, k_tile, turned).astype(BF16)
        one = jnp.where(low, turned, k_tile).astype(BF16)
        return jnp.where(single_low, zero, one), jnp.where(single_low, one, zero)

    def both_pairs(first, last):
        return jnp.where(single_low, first, last), jnp.where(single_low, last, first)

    w_rows = lambda s: wv.at[:, pl.ds(s * 192, 192), :]
    w_piece = lambda s, c: wv.at[c, pl.ds(s * 192, 192), :]
    x_piece = lambda c: wex.at[c]

    def put_w(tile, values):
        wv[tile, pl.ds(seq * 192, 192), :] = values[0]
        wex[tile] = values[1]

    local[0].wait()
    put_w(0, both_pairs(wraw[1, :, tiles[0]], wraw[1, :, tiles[2]]))
    put_w(1, both_singles(wraw[1, :, tiles[1]], wraw[2, :, tiles[1]]))
    put_w(2, both_pairs(wraw[2, :, tiles[0]], wraw[2, :, tiles[2]]))
    put_w(3, both_pairs(wraw[0, :, tiles[0]], wraw[0, :, tiles[2]]))
    put_w(4, [wraw[0, :, tiles[1]]] * 2)

    pl.semaphore_wait(barrier, 15)

    HR = 128 // HC
    h_piece = lambda c: pl.ds(c * HR, HR)
    h_slot = lambda x, h, c: hx.at[x, pl.ds(h * 128 + c * HR, HR), :]

    def hidden_send():
        for k in three:
            send(i_hx[k], hid_h, hx_slot(tp, zh), xdev[k])

    def hidden_own():
        local[1].wait()
        for k in three:
            arrived(i_hx[k], hx_slot(xfrom[k], zh))

    def hidden_cross():
        for c in range(HC):
            send(i_hz[c], hid_h.at[h_piece(c), :], hland.at[h_piece(c), :], zdev)

    def hidden_forward():
        for c in range(HC):
            arrived(i_hz[c], hland.at[h_piece(c), :])
            for k, device in enumerate(xcross + [core]):
                send(i_hf[c][k], hland.at[h_piece(c), :], h_slot(tp, oh, c), device)

    def hidden_other():
        for c in range(HC):
            for k in range(4):
                arrived(i_hf[c][k], h_slot((xfrom + [tp])[k], oh, c))

    def hidden_sent():
        for c in range(HC):
            sent(i_hz[c], hid_h.at[h_piece(c), :])
            for k in range(4):
                sent(i_hf[c][k], hland.at[h_piece(c), :])

    def weights_send(index, src, dst, device, c):
        return pltpu.make_async_remote_copy(
            src_ref=src,
            dst_ref=dst,
            send_sem=send_sem.at[index],
            recv_sem=recv_sem.at[i_ch[c]],
            device_id=device,
            device_id_type=MESH,
        )

    def weights_cross():
        @pl.when(depth == 0)
        def _():
            for c in range(NC):
                weights_send(i_ex[c], x_piece(c), w_piece(seq, c), cross_dev, c).start()

    def weights_y():
        for k in three:
            send(i_wy[k], w_rows(seq), w_rows(seq), ydev[k])

    oseq = oh * 4 + y

    def weights_pass(c):
        arrived(i_ch[c], w_piece(oseq, c))

        @pl.when(depth == 1)
        def _():
            piece = w_piece(oseq, c)
            for k in three:
                weights_send(i_ps[c][k], piece, piece, pass_dev[k], c).start()

    def weights_relay(c):
        for k in three:
            send(i_wr[c][k], w_piece(oseq, c), w_piece(oseq, c), ydev[k])

    def weights_near():
        for k in three:
            arrived(i_wy[k], w_rows(zh * 4 + yfrom[k]))

    def weights_far(c):
        for k in three:
            arrived(i_wr[c][k], w_piece(oh * 4 + yfrom[k], c))

    def weights_sent():
        @pl.when(depth == 0)
        def _():
            for c in range(NC):
                sent(i_ex[c], x_piece(c))

        @pl.when(depth == 1)
        def _():
            for c in range(NC):
                for k in three:
                    sent(i_ps[c][k], w_piece(oseq, c))

        for k in three:
            sent(i_wy[k], w_rows(seq))
            for c in range(NC):
                sent(i_wr[c][k], w_piece(oseq, c))

    st_slot = lambda v, h: kvs.at[v, half_rows(h), :]

    def stale_tiles():
        local[2].wait()

        def put(tile, values):
            kvs[y, half_rows(zh), tiles[tile]] = values[0]
            sex[:, tiles[tile]] = values[1]

        put(0, both_pairs(straw[0, :, tiles[0]], straw[0, :, tiles[2]]))
        put(1, both_singles(straw[0, :, tiles[1]], straw[1, :, tiles[1]]))
        put(2, both_pairs(straw[1, :, tiles[0]], straw[1, :, tiles[2]]))

    def text_tiles():
        local[3].wait()
        tx[144:256, :] = jnp.zeros((112, 384), BF16)
        live = slice(0, txraw.shape[0])
        tx[live, tiles[0]] = both_pairs(txraw[:, 0, tiles[0]], txraw[:, 0, tiles[2]])[0]
        tx[live, tiles[1]] = both_singles(txraw[:, 0, tiles[1]], txraw[:, 1, tiles[1]])[0]
        tx[live, tiles[2]] = both_pairs(txraw[:, 1, tiles[0]], txraw[:, 1, tiles[2]])[0]

    def stale_z():
        send(i_sz, sex, st_slot(y, zh), zdev)

    def stale_y():
        for k in three:
            send(i_sy[k], st_slot(y, zh), st_slot(y, zh), ydev[k])

    def stale_relay():
        arrived(i_sz, st_slot(y, oh))
        for k in three:
            send(i_sr[k], st_slot(y, oh), st_slot(y, oh), ydev[k])

    def stale_all():
        for k in three:
            arrived(i_sy[k], st_slot(yfrom[k], zh))
            arrived(i_sr[k], st_slot(yfrom[k], oh))

    def stale_sent():
        sent(i_sz, sex)
        for k in three:
            sent(i_sy[k], st_slot(y, zh))
            sent(i_sr[k], st_slot(y, oh))

    def out_send(part):
        for k in three:
            send(i_wo[part][k], wo_h.at[wo_part(0, part), :], wo_rows(tp, part), xdev[k])

    def out_all():
        local[11].wait()
        for k in three:
            for part in range(2):
                arrived(i_wo[part][k], wo_rows(xfrom[k], part))

    def norm_rows(r0, count, shift, scale, store):
        parts = [hx[c, pl.ds(r0, count), :].astype(F32) for c in range(4)]
        total = sum(jnp.sum(part, axis=-1, keepdims=True) for part in parts)
        mean = total * (1.0 / 1536)
        parts = [part - mean for part in parts]
        spread = sum(jnp.sum(part * part, axis=-1, keepdims=True) for part in parts)
        inv = lax.rsqrt(spread * (1.0 / 1536) + 1e-06)
        for c in range(4):
            lanes = slice(c * 384, (c + 1) * 384)
            store(c, (parts[c] * inv * (1.0 + scale(lanes)) + shift(lanes)).astype(BF16))

    def norm_block(h):
        for b in range(4):
            r0 = h * 128 + b * 32

            def store(c, value, r0=r0):
                nm[c // 2, pl.ds(r0, 32), (c % 2) * 384 : (c % 2) * 384 + 384] = value

            norm_rows(r0, 32, lambda l: mod[0, :, l], lambda l: mod[1, :, l], store)

    def go(index):
        pl.semaphore_signal(go_sem.at[index], inc=1, device_id=core, device_id_type=MESH)

    def go_wait(index):
        pl.semaphore_wait(go_sem.at[index], 1)

    @pl.when(sec == 0)
    def _():
        weights_cross()
        hidden_send()
        weights_y()

    @pl.when(sec == 1)
    def _():
        hidden_cross()
        out_send(0)

    stale_tiles()
    for copy in local[4:11]:
        copy.wait()

    @pl.when(sec == 0)
    def _():
        send(i_wf, wf.at[0], wf.at[1], core)
        for c in range(NC):
            weights_pass(c)
            weights_relay(c)
        stale_z()
        out_send(0)
        out_send(1)
        stale_y()
        hidden_own()
        norm_block(zh)
        text_tiles()
        hidden_other()
        norm_block(oh)

    @pl.when(sec == 1)
    def _():
        text_tiles()
        hidden_forward()
        go_wait(0)
        stale_z()
        weights_cross()

        @pl.when(depth == 1)
        def _():
            for c in range(NC):
                weights_pass(c)

        go_wait(1)
        weights_y()
        stale_y()

        @pl.when(depth != 1)
        def _():
            for c in range(NC):
                arrived(i_ch[c], w_piece(oseq, c))

        for c in range(NC):
            weights_relay(c)
        stale_relay()
        go_wait(2)
        out_send(1)
        for n in range(4):
            arrived(i_h1[0][n], hx.at[n, half_rows(zh), :])
        norm_block(zh)
        for n in range(4):
            arrived(i_h1[1][n], hx.at[n, half_rows(oh), :])
        norm_block(oh)

    segment = lax.broadcasted_iota(jnp.int32, (1, 256), 1) // 32
    rank_of = [
        [sum(jnp.where(order[k, s] == p, k, 0) for k in range(1, MICRO)) for p in range(MICRO)]
        for s in range(8)
    ]
    row_segment = lax.broadcasted_iota(jnp.int32, (256, 1), 0) // 32
    qrank = jnp.zeros((256, 1), jnp.int32)
    kranks = []
    for v in range(4):
        krank = jnp.zeros((1, 256), jnp.int32)
        for j in range(8):
            scalar = rank_of[(j // 4) * 4 + v][j % 4]
            krank = jnp.where(segment == j, scalar, krank)
            qrank = jnp.where((row_segment == j) & (y == v), scalar, qrank)
        kranks.append(krank)
    text_live = lax.broadcasted_iota(jnp.int32, (1, 256), 1) < tlen[0]

    weights_near()
    for c in range(5):
        acc[:, tiles[c]] = dot(nm[zh], wv[c, pl.ds(zh * 768, 768), :])
    kv_tile = lambda v, c: kvf.at[v, :, tiles[c]]
    for c in range(5):
        weights_far(c)
        value = acc[:, tiles[c]] + dot(nm[oh], wv[c, pl.ds(oh * 768, 768), :])
        if c < 3:
            kvf[y, :, tiles[c]] = value.astype(BF16)
        else:
            lhs[:, tiles[c - 3]] = value.astype(BF16)
        if c < 3:
            for k in three:
                send(i_kv[c][k], kv_tile(y, c), kv_tile(y, c), ydev[k])
    send(i_nk, kvf.at[y, half_rows(oh), :], nkv, zdev)

    @pl.when(sec == 0)
    def _():
        go(0)
        stale_relay()

    stale_all()
    for c in range(3):
        for k in three:
            arrived(i_kv[c][k], kv_tile(yfrom[k], c))

    @pl.when(sec == 0)
    def _():
        go(1)

    def attend(rb):
        rows = half_rows(rb)
        rank = jnp.where(rb == 0, qrank[0:128], qrank[128:256])
        masks = [kranks[v] <= rank for v in range(4)]
        outs = []
        for j in range(3):
            tile = 0 if j < 2 else 1
            query = lhs[rows, tiles[tile]].astype(F32) * (HEAD ** (-0.5))
            if j == 0:
                keep = low
            elif j == 1:
                keep = jnp.logical_not(low)
            else:
                keep = low == single_low
            query = jnp.where(keep, query, 0.0).astype(BF16)
            kl = tiles[tile]
            vl = tiles[2] if j < 2 else kl
            for v in range(4):
                fresh = dot_nt(query, kvf[v, :, kl])
                stale = dot_nt(query, kvs[v, :, kl])
                sbuf[:, v * 256 : v * 256 + 256] = jnp.where(masks[v], fresh, stale)
            text = dot_nt(query, tx[:, kl])
            sbuf[:, 1024:1280] = jnp.where(text_live, text, -1e30)
            scores = sbuf[...]
            peak = jnp.max(scores, axis=-1, keepdims=True)
            weights = jnp.exp(scores - peak)
            inv = 1.0 / jnp.sum(weights, axis=-1, keepdims=True)
            sbuf[...] = weights * inv
            total = dot(sbuf[:, 1024:1280].astype(BF16), tx[:, vl])
            for v in range(4):
                weights = sbuf[:, v * 256 : v * 256 + 256]
                fresh = jnp.where(masks[v], weights, 0.0).astype(BF16)
                stale = jnp.where(masks[v], 0.0, weights).astype(BF16)
                total = total + dot(fresh, kvf[v, :, vl]) + dot(stale, kvs[v, :, vl])
            outs.append(total)
        at[zh, tp, rb, 0:128, :] = jnp.where(low, outs[0], outs[1]).astype(BF16)
        single = jnp.where(low == single_low, 0.0, outs[2])
        single = single + pltpu.roll(single, HEAD, 1)
        at[zh, tp, rb, 128:192, :] = jnp.where(low, single[0:64], single[64:128]).astype(BF16)

    block = lambda a, x, rb: at.at[a, x, rb]
    attend(oh)
    send(i_az[0], block(zh, tp, oh), block(zh, tp, oh), zdev)

    @pl.when(sec == 0)
    def _():
        for k in three:
            send(i_ax[1][k], block(zh, tp, oh), block(zh, tp, oh), xdev[k])

    attend(zh)

    @pl.when(sec == 0)
    def _():
        send(i_az[1], block(zh, tp, zh), block(zh, tp, zh), zdev)

    for k in three:
        send(i_ax[0][k], block(zh, tp, zh), block(zh, tp, zh), xdev[k])

    arrived(i_nk, nkv)
    mine_kv = [kvf[y, half_rows(zh), tiles[c]] for c in range(3)]
    their_kv = [nkv[:, tiles[c]] for c in range(3)]
    first_kv = [jnp.where(single_low, a, b) for a, b in zip(mine_kv, their_kv)]
    second_kv = [jnp.where(single_low, b, a) for a, b in zip(mine_kv, their_kv)]
    out_kv[0, :, tiles[0]] = first_kv[0]
    out_kv[0, :, tiles[1]] = jnp.where(low, first_kv[1], second_kv[1])
    out_kv[0, :, tiles[2]] = second_kv[0]
    out_kv[1, :, tiles[0]] = first_kv[2]
    out_kv[1, :, tiles[1]] = turn(jnp.where(low, second_kv[1], first_kv[1])).astype(BF16)
    out_kv[1, :, tiles[2]] = second_kv[2]

    arrived(i_az[0], block(oh, tp, zh))
    for k in three:
        send(i_af[0][k], block(oh, tp, zh), block(oh, tp, zh), xdev[k])

    @pl.when(sec == 0)
    def _():
        arrived(i_az[1], block(oh, tp, oh))
        for k in three:
            send(i_af[1][k], block(oh, tp, oh), block(oh, tp, oh), xdev[k])
        for k in three:
            sent(i_hx[k], hid_h)

    def out_rows(part, rb):
        for k in three:
            arrived(i_ax[part][k], block(zh, xfrom[k], rb))
        for k in three:
            arrived(i_af[part][k], block(oh, xfrom[k], rb))
        for x in range(4):
            lhs[0:128, tiles[3 * x]] = at[0, x, rb, 0:128, :]
            lhs[0:128, tiles[3 * x + 2]] = at[1, x, rb, 0:128, :]
            a = at[0, x, rb, 128:192, :]
            b = at[1, x, rb, 128:192, :]
            lhs[0:64, tiles[3 * x + 1]] = jnp.where(low, a.astype(F32), turn(b)).astype(BF16)
            lhs[64:128, tiles[3 * x + 1]] = jnp.where(low, turn(a), b.astype(F32)).astype(BF16)
        for n in range(4):
            lanes = slice(n * 384, n * 384 + 384)
            branch = dot(lhs[0:128, :], wo[:, lanes])
            rows = half_rows(rb)
            hx[n, rows, :] = (hx[n, rows, :].astype(F32) + mod[2, :, lanes] * branch).astype(BF16)

            @pl.when(sec == 0)
            def _():
                send(i_h1[part][n], hx.at[n, rows, :], hx.at[n, rows, :], core)

    out_all()
    out_rows(0, zh)

    @pl.when(sec == 0)
    def _():
        out_rows(1, oh)
        go(2)

    @pl.when(sec == 1)
    def _():
        for b in range(4):

            def store(c, value, b=b):
                fin[b * 32 : b * 32 + 32, c * 384 : c * 384 + 384] = value

            norm_rows(
                zh * 128 + b * 32, 32, lambda l: fmod[0:1, l], lambda l: fmod[1:2, l], store
            )
        arrived(i_wf, wf.at[1])
        theirs = dot_nt(wf[1], fin[...])
        vel[0] = theirs
        send(i_fn, vel.at[0], vel.at[1], core)
        out_lat[...] = lat[...] + step[0] * dot_nt(wf[0], fin[...])

    @pl.when(sec == 0)
    def _():
        arrived(i_fn, vel.at[1])
        out_lat[...] = lat[...] + step[0] * vel[1]

    @pl.when(sec == 0)
    def _():
        for part, rb in ((0, zh), (1, oh)):
            for n in range(4):
                sent(i_h1[part][n], hx.at[n, half_rows(rb), :])
        sent(i_wf, wf.at[0])
        sent(i_az[1], block(zh, tp, zh))
        for k in three:
            sent(i_ax[1][k], block(zh, tp, oh))
            sent(i_af[1][k], block(oh, tp, oh))

    @pl.when(sec == 1)
    def _():
        sent(i_fn, vel.at[0])
        hidden_sent()

    weights_sent()
    stale_sent()
    for k in three:
        for part in range(2):
            sent(i_wo[part][k], wo_rows(tp, part))
        for c in range(3):
            sent(i_kv[c][k], kv_tile(y, c))
        sent(i_ax[0][k], block(zh, tp, zh))
        sent(i_af[0][k], block(oh, tp, zh))
    sent(i_nk, nkv)
    sent(i_az[0], block(zh, tp, oh))


def body(
    hidden, latent, w_qkv, w_out, modulation, final_mod, w_final, stale_kv, text_kv, text_len,
    patch_order, step_size,
):
    vmem = pl.BlockSpec(memory_space=pltpu.VMEM)
    any_ = pl.BlockSpec(memory_space=pltpu.HBM)
    text = text_kv[0].transpose(1, 0, 2)
    lat_next, kv_next = pl.pallas_call(
        kernel,
        out_shape=(
            jax.ShapeDtypeStruct((8, 128), F32),
            jax.ShapeDtypeStruct((2, 128, 384), BF16),
        ),
        in_specs=[any_] * 12,
        out_specs=(vmem, vmem),
        scratch_shapes=[
            pltpu.VMEM((4, 256, 384), BF16),
            pltpu.VMEM((128, 384), BF16),
            pltpu.VMEM((3, 192, 384), BF16),
            pltpu.VMEM((5, 192, 128), BF16),
            pltpu.VMEM((5, 1536, 128), BF16),
            pltpu.VMEM((4, 256, 384), BF16),
            pltpu.VMEM((4, 256, 384), BF16),
            pltpu.VMEM((2, 128, 384), BF16),
            pltpu.VMEM((128, 384), BF16),
            pltpu.VMEM(text.shape, BF16),
            pltpu.VMEM((256, 384), BF16),
            pltpu.VMEM((1536, 1536), BF16),
            pltpu.VMEM((2, 256, 768), BF16),
            pltpu.VMEM((2, 4, 2, 192, 128), BF16),
            pltpu.VMEM((256, 1536), BF16),
            pltpu.VMEM((128, 384), BF16),
            pltpu.VMEM((128, 1536), BF16),
            pltpu.VMEM((256, 640), F32),
            pltpu.VMEM((128, 1280), F32),
            pltpu.VMEM((3, 1, 1536), F32),
            pltpu.VMEM((2, 1536), F32),
            pltpu.VMEM((2, 8, 1536), BF16),
            pltpu.VMEM((2, 8, 128), F32),
            pltpu.VMEM((8, 128), F32),
            pltpu.SMEM((4, 8), jnp.int32),
            pltpu.SMEM((1,), jnp.int32),
            pltpu.SMEM((1,), F32),
            pltpu.SemaphoreType.DMA((N_LINK,)),
            pltpu.SemaphoreType.DMA((N_LINK,)),
            pltpu.SemaphoreType.DMA((N_LOCAL,)),
            pltpu.SemaphoreType.REGULAR((3,)),
        ],
        compiler_params=pltpu.CompilerParams(
            collective_id=0, has_side_effects=True, vmem_limit_bytes=48 << 20
        ),
        name="both_layers",
    )(
        *[
            pltpu.with_memory_space_constraint(value, pltpu.HBM) if value.ndim > 1 else value
            for value in (
                patch_order.T, text_len, step_size, hidden, w_qkv[0].transpose(1, 0, 2), w_out[0],
                stale_kv[0], text, modulation.transpose(1, 0, 2), final_mod, w_final.T, latent.T,
            )
        ]
    )
    return lat_next.T, kv_next[None]


def solution(mesh):
    return jax.shard_map(
        body,
        mesh=mesh,
        in_specs=(
            P(("req", "seq"), "tp"),
            P(("req", "seq"), ("section", "tp")),
            P("section", "seq", None, "tp"),
            P("section", "tp", None),
            P("section", None, None),
            P(),
            P(None, ("section", "tp")),
            P("section", None, ("req", "seq"), "tp"),
            P("section", None, "req", "tp"),
            P("req"),
            P("req", None),
            P(),
        ),
        out_specs=(P(("req", "seq"), ("section", "tp")), P("section", None, ("req", "seq"), "tp")),
        check_vma=False,
    )
```
